32 devices in a mesh: bead: 8 (over y, x, core), space: 4 (over z).
Axes of the slice: x: 2, y: 2, z: 4, core: 2. Of those that a mesh axis runs over, the one named last changes fastest.
Arguments:
- positions: float32 [32, 3, 2048], P('bead', None, 'space'), may hold values from -3 to 3
- momenta: float32 [32, 3, 2048], P('bead', None, 'space'), may hold values from -6 to 6
- neighbours: int32 [32, 2048], P(None, 'space'), may hold values from 0 to 767, as said below
- ghost_rows: int32 [1024], P('space'), may hold values from 0 to 511
- species: int32 [2048], P('space'), may hold values from 0 to 1
- species_scale: float32 [2], replicated, may hold values from 0.5 to 2
- mass_table: float32 [2], replicated, may hold values from 0.25 to 1
- w_in: float32 [128, 8], replicated, may hold values from -2 to 2
- w_out: float32 [8, 128], replicated, may hold values from -0.5 to 0.5
Outputs:
- new_positions: float32 [32, 3, 2048], P('bead', None, 'space')
- new_momenta: float32 [32, 3, 2048], P('bead', None, 'space')
The draws below stay inside these ranges and needn't reach their ends.
Inputs may be any that keep to these rules, and one draw needn't show every extreme that they name: `neighbours`: A neighbour entry indexes the window of its atom's domain; slots beyond an atom's live count hold the atom's own position 128 + (atom index mod 512); every atom has at least 8 live slots. `ghost_rows`: domain d's block is entries 2 * 128 * d to 2 * 128 * (d + 1) - 1; entries index atoms within domain d.
All inputs are finite; a program needn't handle non-finite values.
Results may differ from the reference program's by a relative error of at most 0.0003.
Values sent between devices are 32-bit elements; how exact they have to be, the bound alone decides.
A program may use at most 64 MiB of HBM per device.

```python
import math
import jax
import jax.numpy as jnp
import numpy as np
from jax import lax

BEADS = 32
CB = 4
SPECIES = 2
H = 128
NRBF = 8
SLOTS = 32
NINNER = 3
ATOM_DEV = 512
GHOST = 128
ATOMS = 2048
GHOST_ROWS = 1024
N_SPACE = 4


def draw_neighbours(key, part):
    first_key = jax.random.fold_in(key, 11)
    second_key = jax.random.fold_in(key, 23)
    counts = jax.random.randint(first_key, (1, ATOMS), SLOTS // 4, SLOTS + 1)
    picks = jax.random.randint(second_key, (SLOTS, ATOMS), 0, ATOM_DEV + 2 * GHOST)
    slot_ids = jnp.arange(SLOTS, dtype=jnp.int32)[:, None]
    itself = GHOST + jnp.arange(ATOMS, dtype=jnp.int32) % ATOM_DEV
    return jnp.where(slot_ids < counts, picks, itself[None, :]).astype(jnp.int32)


def touch_ends(entries, stream_key, least, high):
    extent = entries.shape
    index_at = [jax.random.randint(jax.random.fold_in(stream_key, axis), (), 0, extent[axis]) for axis in range(len(extent))]
    entries = entries.at[tuple(index_at)].set(least)
    longest = extent.index(max(extent))
    index_at[longest] = (index_at[longest] + 1) % extent[longest]
    return entries.at[tuple(index_at)].set(high)


def levels(key, extent, split, smallest, largest):
    factor_of = 1.0
    for axis_at, shards_of in split:
        steps = jax.random.uniform(jax.random.fold_in(jax.random.fold_in(key, 6), axis_at), (shards_of,), jnp.float32, smallest / len(split), largest / len(split))
        factor_of = factor_of * jnp.repeat(jnp.exp(steps), extent[axis_at] // shards_of).reshape((-1,) + (1,) * (len(extent) - 1 - axis_at))
    return factor_of


def bell_draw(own_key, shape, width, bound, pieces=(), held_as=jnp.bfloat16):
    drawn = width * jax.random.normal(own_key, shape, jnp.float32)
    if pieces:
        drawn = drawn * levels(own_key, shape, pieces, -0.22, 0.18)
    return jnp.clip(drawn, -bound, bound).astype(held_as)


def setup_inputs(seed: int = 0) -> dict:
    key_list = jax.random.split(jax.random.key(seed), 10)
    positions = bell_draw(key_list[0], (BEADS, 3, ATOMS), 0.5, 3.0, ((0, 8), (2, 4)), jnp.float32)
    momenta = bell_draw(key_list[1], (BEADS, 3, ATOMS), 1.0, 6.0, ((0, 8), (2, 4)), jnp.float32)
    neighbours = draw_neighbours(jax.random.fold_in(key_list[9], 71), 0)
    ghost_rows = touch_ends(jax.random.randint(key_list[3], (GHOST_ROWS,), 0, ATOM_DEV), jax.random.fold_in(key_list[3], 1), 0, ATOM_DEV - 1).astype(jnp.int32)
    species = touch_ends(jax.random.randint(key_list[4], (ATOMS,), 0, SPECIES), jax.random.fold_in(key_list[4], 1), 0, SPECIES - 1).astype(jnp.int32)
    species_scale = jnp.clip(jnp.exp(jax.random.uniform(key_list[5], (SPECIES,), jnp.float32, math.log(0.5), math.log(2.0))), 0.5, 2.0)
    mass_table = jnp.clip(jnp.exp(jax.random.uniform(key_list[6], (SPECIES,), jnp.float32, math.log(0.25), math.log(1.0))), 0.25, 1.0)
    w_in = bell_draw(key_list[7], (H, NRBF), NRBF ** -0.5, 2.0, (), jnp.float32)
    w_out = bell_draw(key_list[8], (NRBF, H), H ** -0.5, 0.5, (), jnp.float32)
    return dict(positions=positions, momenta=momenta, neighbours=neighbours, ghost_rows=ghost_rows, species=species, species_scale=species_scale, mass_table=mass_table, w_in=w_in, w_out=w_out)


polymer_freq = 10.0
outer_step = 6.0
pair_width = 1.0
pair_strength = 1.0
highest = lax.Precision.HIGHEST

def mode_matrix(count):
    beadpos = np.arange(count)[None, :]
    modeidx = np.arange(count)[:, None]
    middle = count // 2
    cosine = np.sqrt(2.0 / count) * np.cos(2.0 * np.pi * beadpos * modeidx / count)
    sine_rows = np.sqrt(2.0 / count) * np.sin(2.0 * np.pi * beadpos * modeidx / count)
    matrix = np.where(modeidx < middle, cosine, sine_rows)
    matrix = np.where(modeidx == 0, 1.0 / np.sqrt(count), matrix)
    matrix = np.where(modeidx == middle, np.cos(np.pi * beadpos) / np.sqrt(count), matrix)
    return matrix

def mode_scales(count, inner_step):
    frequency = 2.0 * polymer_freq * np.sin(np.pi * np.arange(count) / count)
    nonzero = np.where(frequency > 0, frequency, 1.0)
    cosine = np.cos(frequency * inner_step)
    drift_gain = np.where(frequency > 0, np.sin(frequency * inner_step) / nonzero, inner_step)
    spring = frequency * np.sin(frequency * inner_step)
    return (cosine, drift_gain, spring)

def polymer_tables(count, inner_step):
    modes = mode_matrix(count)
    cosine, drift_gain, spring = mode_scales(count, inner_step)
    persist = modes.T @ (cosine[:, None] * modes)
    coupling = modes.T @ (drift_gain[:, None] * modes)
    restoring = -(modes.T @ (spring[:, None] * modes))
    return (jnp.asarray(persist, jnp.float32), jnp.asarray(coupling, jnp.float32), jnp.asarray(restoring, jnp.float32))

def contraction(count, fewer):
    full_modes = mode_matrix(count)
    small_modes = mode_matrix(fewer)
    kept = list(range(fewer // 2 + 1)) + list(range(count - fewer // 2 + 1, count))
    contract = np.sqrt(fewer / count) * (small_modes.T @ full_modes[kept])
    expand = count / fewer * contract.T
    return (jnp.asarray(contract, jnp.float32), jnp.asarray(expand, jnp.float32))

def radial_rates(count):
    return 0.2 * 2.0 ** (np.arange(count) / 2.0)

def species_lookup(species, table):
    kinds = jnp.arange(table.shape[0], dtype=jnp.int32)
    return lax.optimization_barrier(jnp.sum(jnp.where(species[None, :] == kinds[:, None], table[:, None], 0.0), axis=0))

def pair_forces(extended, targets, centres):
    others = extended[:, targets]
    middle = extended[:, centres]
    offsets = others[:3] - middle[:3, None, :]
    squared = lax.optimization_barrier(jnp.sum(offsets * offsets, axis=0))
    weights = others[3] * jnp.exp(-squared / pair_width)
    return pair_strength * middle[3] * lax.optimization_barrier(jnp.sum(weights[None] * offsets, axis=1))

def learned_forces(extended, charges, targets, centres, w_in, w_out):
    live = (targets != centres[None, :]).astype(jnp.float32)
    weights = charges[targets] * live
    others = extended[:, targets]
    middle = extended[:, centres]
    offsets = others - middle[:, None, :]
    squared = lax.optimization_barrier(jnp.sum(offsets * offsets, axis=0))
    rates = jnp.asarray(radial_rates(w_in.shape[1]), jnp.float32)
    basis = jnp.exp(-rates[:, None, None] * squared[None])
    message = lax.optimization_barrier(jnp.sum(weights[None] * basis, axis=1)) / targets.shape[0]
    hidden = jax.nn.silu(jnp.dot(w_in, message, precision=highest, preferred_element_type=jnp.float32))
    radial = jnp.dot(w_out, hidden, precision=highest, preferred_element_type=jnp.float32)
    profile = lax.optimization_barrier(jnp.sum(radial[:, None, :] * basis, axis=0))
    return lax.optimization_barrier(jnp.sum((weights * profile)[None] * offsets, axis=1))

def window(values, ghost_rows):
    channels = values.shape[0]
    blocks = values.reshape(channels, N_SPACE, ATOM_DEV)
    picked = ghost_rows.reshape(N_SPACE, 2 * GHOST)
    sends = jnp.take_along_axis(blocks, jnp.broadcast_to(picked[None], (channels, N_SPACE, 2 * GHOST)), axis=2)
    from_below = jnp.roll(sends[:, :, GHOST:], 1, axis=1)
    from_above = jnp.roll(sends[:, :, :GHOST], -1, axis=1)
    return jnp.concatenate([from_below, blocks, from_above], axis=2).reshape(channels, -1)

def reference(positions, momenta, neighbours, ghost_rows, species, species_scale, mass_table, w_in, w_out):
    inner_step = outer_step / NINNER
    persist, coupling, restoring = polymer_tables(BEADS, inner_step)
    contract, expand = contraction(BEADS, CB)
    charges = species_lookup(species, species_scale)
    masses = species_lookup(species, mass_table)
    window_length = ATOM_DEV + 2 * GHOST
    atom_ids = jnp.arange(ATOMS, dtype=jnp.int32)
    domain = atom_ids // ATOM_DEV
    targets = domain[None, :] * window_length + neighbours
    centres = domain * window_length + GHOST + atom_ids % ATOM_DEV
    charge_window = window(charges[None], ghost_rows)[0]

    def cheap_forces(coords):

        def single(bead_coords):
            extended = window(jnp.concatenate([bead_coords, charges[None]], axis=0), ghost_rows)
            return pair_forces(extended, targets, centres)
        return lax.map(single, coords)

    def expensive_forces(coords):
        reduced = jnp.einsum('cb,bxa->cxa', contract, coords, precision=highest)

        def single(reduced_coords):
            return learned_forces(window(reduced_coords, ghost_rows), charge_window, targets, centres, w_in, w_out)
        return jnp.einsum('bc,cxa->bxa', expand, lax.map(single, reduced), precision=highest)

    def propagate(coords, moments):
        new_coords = jnp.einsum('ab,bxn->axn', persist, coords, precision=highest) + jnp.einsum('ab,bxn->axn', coupling, moments, precision=highest) / masses
        new_moments = jnp.einsum('ab,bxn->axn', persist, moments, precision=highest) + jnp.einsum('ab,bxn->axn', restoring, coords, precision=highest) * masses
        return (new_coords, new_moments)
    coords = positions
    moments = momenta + 0.5 * outer_step * expensive_forces(coords)
    cheap_now = cheap_forces(coords)
    for repeat in range(NINNER):
        moments = moments + 0.5 * inner_step * cheap_now
        coords, moments = propagate(coords, moments)
        cheap_now = cheap_forces(coords)
        moments = moments + 0.5 * inner_step * cheap_now
    moments = moments + 0.5 * outer_step * expensive_forces(coords)
    return (coords, moments)
```

```python
import jax
import jax.numpy as jnp
import numpy as np
from jax import lax
from jax.experimental import pallas as pl
from jax.experimental.pallas import tpu as pltpu
from jax.sharding import PartitionSpec as P

BEADS = 32
CB = 4
NINNER = 3


polymer_freq = 10.0
outer_step = 6.0
pair_width = 1.0
pair_strength = 1.0
highest = lax.Precision.HIGHEST


def mode_matrix(count):
    beadpos = np.arange(count)[None, :]
    modeidx = np.arange(count)[:, None]
    middle = count // 2
    cosine = np.sqrt(2.0 / count) * np.cos(2.0 * np.pi * beadpos * modeidx / count)
    sine_rows = np.sqrt(2.0 / count) * np.sin(2.0 * np.pi * beadpos * modeidx / count)
    matrix = np.where(modeidx < middle, cosine, sine_rows)
    matrix = np.where(modeidx == 0, 1.0 / np.sqrt(count), matrix)
    matrix = np.where(modeidx == middle, np.cos(np.pi * beadpos) / np.sqrt(count), matrix)
    return matrix


def mode_scales(count, inner_step):
    frequency = 2.0 * polymer_freq * np.sin(np.pi * np.arange(count) / count)
    nonzero = np.where(frequency > 0, frequency, 1.0)
    cosine = np.cos(frequency * inner_step)
    drift_gain = np.where(frequency > 0, np.sin(frequency * inner_step) / nonzero, inner_step)
    spring = frequency * np.sin(frequency * inner_step)
    return (cosine, drift_gain, spring)


def contraction(count, fewer):
    full_modes = mode_matrix(count)
    small_modes = mode_matrix(fewer)
    kept = list(range(fewer // 2 + 1)) + list(range(count - fewer // 2 + 1, count))
    contract = np.sqrt(fewer / count) * (small_modes.T @ full_modes[kept])
    expand = count / fewer * contract.T
    return (contract, expand)


def radial_rates(count):
    return 0.2 * 2.0 ** (np.arange(count) / 2.0)

LANES = 128
TILE = 8
KINDS = 5
MESH = pl.DeviceIdType.MESH


def layout(devices, per_device, atoms):
    groups_of = TILE // per_device
    halves = min(atoms // LANES, groups_of)
    return groups_of, halves, atoms // (halves * LANES)


def tables(devices, per_device, atoms):
    inner_step = outer_step / NINNER
    groups_of, halves, _ = layout(devices, per_device, atoms)
    modes = mode_matrix(BEADS)
    contract, expand = contraction(BEADS, CB)
    kick = 0.5 * outer_step * expand

    def power(count):
        cosine, drift_gain, spring = mode_scales(BEADS, inner_step)
        step = np.zeros((2 * BEADS, 2 * BEADS))
        step[:BEADS, :BEADS] = step[BEADS:, BEADS:] = modes.T @ (cosine[:, None] * modes)
        step[:BEADS, BEADS:] = modes.T @ (drift_gain[:, None] * modes)
        step[BEADS:, :BEADS] = -(modes.T @ (spring[:, None] * modes))
        whole = np.linalg.matrix_power(step, count)
        return (whole[:BEADS, :BEADS], whole[:BEADS, BEADS:], whole[BEADS:, :BEADS], whole[BEADS:, BEADS:])

    powers = [power(count) for count in range(NINNER + 1)]
    width = devices * TILE
    extra = halves * CB
    total = -(-(width + extra) // LANES) * LANES
    beads = np.arange(BEADS)
    column = beads // per_device * TILE + beads % per_device

    def block(matrix, device):
        out = np.zeros((TILE, width))
        for q in range(groups_of):
            for b in range(per_device):
                out[q * per_device + b, column + q * per_device] = matrix[device * per_device + b]
        return out

    def member_block(row):
        out = np.zeros((TILE, width))
        for q in range(groups_of):
            out[q, column + q * per_device] = row
        return out

    def piece_block(matrix, device):
        out = np.zeros((TILE, extra))
        for q in range(halves):
            for b in range(per_device):
                out[q * per_device + b, q * CB : (q + 1) * CB] = matrix[device * per_device + b]
        return out

    def piece_member_block(row):
        out = np.zeros((TILE, extra))
        for q in range(halves):
            out[q, q * CB : (q + 1) * CB] = row
        return out

    result = []
    for device in range(devices):
        chosen = contract[device // (devices // CB)]
        rows = []

        def add(left, right=None):
            line = np.zeros((left.shape[0], total))
            line[:, : left.shape[1]] = left
            if right is not None:
                line[:, width : width + extra] = right
            rows.append(line)

        share = np.zeros((CB * halves, TILE))
        for c in range(CB):
            for h in range(halves):
                for b in range(per_device):
                    share[c * halves + h, h * per_device + b] = contract[c, device * per_device + b]
        add(share)
        add(piece_block(kick, device))
        for count in range(1, NINNER + 1):
            add(block(powers[count][0], device))
        add(block(powers[NINNER][2], device))
        add(member_block(chosen @ powers[NINNER][0]))
        for start in range(NINNER):
            for count in range(1, NINNER + 1 - start):
                add(block(powers[count][1], device), piece_block(powers[count][1] @ kick, device))
            last = powers[NINNER - start]
            add(block(last[3], device), piece_block(last[3] @ kick, device))
            add(member_block(chosen @ last[1]), piece_member_block(chosen @ last[1] @ kick))
        result.append(np.concatenate(rows, axis=0))
    return jnp.asarray(np.stack(result), jnp.float32)


def dot(a, b):
    return jnp.dot(a, b, precision=highest, preferred_element_type=jnp.float32)


def lookup(chunk, low):
    return jnp.take_along_axis(chunk, low, axis=1, mode="promise_in_bounds")


def pick(chunks, low, high):
    found = None
    for number, chunk in enumerate(chunks):
        value = lookup(chunk, low)
        found = value if found is None else jnp.where(high == number, value, found)
    return found


def cycle_kernel(
    pos_in, mom_in, near_in, ghost_from, species_in, scale_in, mass_in, w_in_in, w_out_in, table_in,
    new_pos_ref, new_mom_ref,
    first_pos, first_vel, inv_ref, factor_ref, mass_rows, weight, kick, acc, ghost_acc,
    begin, kicks, zg_out, zg_in, part_line, part_out, part_in, q_own, qg_out, qg_in, piece,
    free_out, free_in, edge_out, edge_in,
    pos_ref, mom_ref, near_ref, ghost_ref, species_ref, scale_ref, mass_ref, w_in_ref, w_out_ref,
    table_ref, load_s, zg_s, zg_r, part_s, part_r, begin_s, begin_r, qg_s, qg_r, kick_s, kick_r,
    piece_s, piece_r, free_s, free_r, edge_s, edge_r,
):
    _, per_device, atoms = pos_ref.shape
    slots = near_ref.shape[0]
    ghosts = ghost_ref.shape[1]
    devices = lax.axis_size("bead")
    domains = lax.axis_size("space")
    me = lax.axis_index("bead")
    domain = lax.axis_index("space")
    above = lax.rem(domain + 1, domains)
    below = lax.rem(domain + domains - 1, domains)
    inner_step = outer_step / NINNER
    groups_of, halves, strips = layout(devices, per_device, atoms)
    wide = 3 * LANES
    used = halves * per_device
    ghost_tiles = -(-3 // groups_of)
    groups = devices // CB
    share = atoms // groups
    cover = max(share, LANES)
    member = me // groups
    first = lax.rem(me, groups) * share // LANES * LANES
    atom_chunks = atoms // LANES
    width = devices * TILE
    extra = halves * CB

    def partner(j):
        at, bit = me, 1
        while bit < devices:
            if j & bit:
                at = at + bit - 2 * bit * lax.rem(at // bit, 2)
            bit *= 2
        return at

    peers = [partner(j) for j in range(devices)]
    order = list(range(devices - 1, 0, -1))

    pairs = (
        (pos_in, pos_ref), (mom_in, mom_ref), (species_in, species_ref), (scale_in, scale_ref),
        (mass_in, mass_ref), (ghost_from, ghost_ref), (table_in.at[me], table_ref),
        (near_in, near_ref), (w_in_in, w_in_ref), (w_out_in, w_out_ref),
    )
    loads = [
        pltpu.make_async_copy(src, dst, load_s.at[number])
        for number, (src, dst) in enumerate(pairs)
    ]
    for load in loads:
        load.start()
    barrier = pltpu.get_barrier_semaphore()
    for j in order:
        pl.semaphore_signal(barrier, inc=1, device_id={"bead": peers[j]}, device_id_type=MESH)
    for target in (above, below):
        pl.semaphore_signal(barrier, inc=1, device_id={"space": target}, device_id_type=MESH)

    def to_peer(src, dst, send, recv, j):
        return pltpu.make_async_remote_copy(
            src_ref=src, dst_ref=dst, send_sem=send.at[j], recv_sem=recv.at[j],
            device_id={"bead": peers[j]}, device_id_type=MESH,
        )

    def to_side(src, dst, send, recv, side):
        return pltpu.make_async_remote_copy(
            src_ref=src, dst_ref=dst, send_sem=send.at[side], recv_sem=recv.at[side],
            device_id={"space": (above, below)[side]}, device_id_type=MESH,
        )

    def to_edge(step, side, j, sender):
        return pltpu.make_async_remote_copy(
            src_ref=edge_out.at[step, side], dst_ref=edge_in.at[step, side, sender],
            send_sem=edge_s.at[step, side, j], recv_sem=edge_r.at[step, side, j],
            device_id={"bead": peers[j], "space": (above, below)[side]}, device_id_type=MESH,
        )

    sent = []

    def start(copies):
        for copy in copies:
            copy.start()
            sent.append(copy)

    def await_blocks(buffer, send, recv):
        for j in order:
            to_peer(buffer.at[peers[j]], buffer.at[peers[j]], send, recv, j).wait_recv()

    row_at = lax.broadcasted_iota(jnp.int32, (TILE, LANES), 0)

    def spread_row(row):
        return jnp.broadcast_to(row, (TILE, LANES))

    def lane_of(strip, c):
        at = (strip * 3 + c) * LANES
        return slice(at, at + LANES)

    def chunk_of(m):
        return slice(m * LANES, (m + 1) * LANES)

    def fold(value, unit):
        shift = unit
        while shift < TILE:
            value = value + pltpu.roll(value, shift, 0)
            shift *= 2
        return value

    def index_of(side):
        index = spread_row(ghost_ref[1 - side : 2 - side, :])
        return index & (LANES - 1), index // LANES

    def ghost_values(ref, lead, side, unit):
        low, high = index_of(side)
        half = high // strips
        strip_at = high - half * strips
        values = []
        for c in range(3):
            parts = [lookup(ref[(*lead, slice(None), lane_of(s, c))], low) for s in range(strips)]
            value = parts[0]
            for s in range(1, strips):
                value = jnp.where(strip_at == s, parts[s], value)
            value = jnp.where(row_at // unit == half, value, 0.0)
            values.append(fold(value, unit))
        return values

    def compose(values, unit):
        tiles = []
        for t in range(ghost_tiles):
            tile = jnp.zeros((TILE, LANES), jnp.float32)
            for c in range(t * groups_of, min(len(values), (t + 1) * groups_of)):
                tile = jnp.where(row_at // unit == c % groups_of, values[c], tile)
            tiles.append(tile)
        return tiles

    for load in loads[:7]:
        load.wait()
    species = species_ref[...]
    charge = jnp.zeros((1, atoms), jnp.float32)
    mass = jnp.zeros((1, atoms), jnp.float32)
    for kind in range(scale_ref.shape[1]):
        charge = jnp.where(species == kind, scale_ref[0:1, kind : kind + 1], charge)
        mass = jnp.where(species == kind, mass_ref[0:1, kind : kind + 1], mass)
    inverse = 1.0 / mass
    factor_ref[...] = charge * inverse

    if used < TILE:
        first_pos[...] = jnp.zeros(first_pos.shape, jnp.float32)
        first_vel[...] = jnp.zeros(first_vel.shape, jnp.float32)
        kick[...] = jnp.zeros(kick.shape, jnp.float32)
        inv_ref[...] = jnp.zeros(inv_ref.shape, jnp.float32)
        mass_rows[...] = jnp.zeros(mass_rows.shape, jnp.float32)
    for h in range(halves):
        at = slice(h * per_device, (h + 1) * per_device)
        for s in range(strips):
            chunk = chunk_of(h * strips + s)
            for c in range(3):
                first_pos[at, lane_of(s, c)] = pos_ref[c, :, chunk]
    begin[me] = first_pos[...]
    charge_ghosts = []
    for side in range(2):
        low, high = index_of(side)
        parts = [spread_row(charge[:, chunk_of(m)]) for m in range(atom_chunks)]
        values = ghost_values(first_pos, (), side, per_device) + [pick(parts, low, high)]
        for t, tile in enumerate(compose(values, per_device)):
            zg_out[0, side, t * TILE : (t + 1) * TILE, :] = tile

    part_line[0:extra, :] = dot(table_ref[0:extra, 0:TILE], first_pos[...])
    for c in range(CB):
        for i in range(3):
            for m in range(atom_chunks):
                h, s = m // strips, m % strips
                row = c * halves + h
                at = i * atom_chunks + m
                part_out[c, at : at + 1, :] = part_line[row : row + 1, lane_of(s, i)]

    pl.semaphore_wait(barrier, devices + 1)
    ghost_copies = [
        to_side(zg_out.at[0, side], zg_in.at[0, side], zg_s.at[0], zg_r.at[0], side)
        for side in range(2)
    ]
    start(ghost_copies)
    start([to_peer(part_out.at[peers[j] // groups], part_in.at[me], part_s, part_r, j) for j in order])
    start([to_peer(begin.at[me], begin.at[me], begin_s, begin_r, j) for j in order])

    for h in range(halves):
        at = slice(h * per_device, (h + 1) * per_device)
        for s in range(strips):
            chunk = chunk_of(h * strips + s)
            own = jnp.broadcast_to(inverse[:, chunk], (per_device, LANES))
            inv_ref[at, chunk_of(s)] = own
            mass_rows[at, chunk_of(s)] = jnp.broadcast_to(mass[:, chunk], (per_device, LANES))
            for c in range(3):
                first_vel[at, lane_of(s, c)] = mom_ref[c, :, chunk] * own

    await_blocks(part_in, part_s, part_r)
    contracted = part_out[member]
    for j in order:
        contracted = contracted + part_in[peers[j]]
    part_line[0 : contracted.shape[0], 0:LANES] = contracted

    def put_q(value_of):
        for i in range(3):
            for m in range(atom_chunks):
                q_own[i : i + 1, chunk_of(m)] = value_of(i, m)

    put_q(lambda i, m: part_line[i * atom_chunks + m : i * atom_chunks + m + 1, 0:LANES])
    for side in range(2):
        low, high = index_of(side)
        qg_out[side] = pick([q_own[:, chunk_of(m)] for m in range(atom_chunks)], low, high)
    qcopies = [to_side(qg_out.at[side], qg_in.at[side], qg_s, qg_r, side) for side in range(2)]
    start(qcopies)
    for load in loads[7:]:
        load.wait()
    for copy in ghost_copies:
        copy.wait_recv()

    def ghost_row(ref, lead, side, c, b):
        at = c // groups_of * TILE + c % groups_of * per_device + b
        return spread_row(ref[(*lead, side, slice(at, at + 1), slice(None))])

    chunks = [ghost_row(zg_in, (0,), 0, 3, 0)]
    chunks += [spread_row(charge[:, chunk_of(m)]) for m in range(atom_chunks)]
    chunks += [ghost_row(zg_in, (0,), 1, 3, 0)]
    for m in range(atom_chunks):
        itself = ghosts + m * LANES + lax.broadcasted_iota(jnp.int32, (TILE, LANES), 1)
        for k in range(0, slots, TILE):
            index = near_ref[k : k + TILE, chunk_of(m)]
            value = pick(chunks, index & (LANES - 1), index // LANES)
            weight[k : k + TILE, chunk_of(m)] = jnp.where(index == itself, 0.0, value)

    def cheap(own_ref, own_lead, ghost_ref_of, ghost_lead, finish):
        for s in range(strips):
            for h in range(halves):
                lanes = chunk_of(h * strips + s)
                factor = factor_ref[:, lanes]
                indices = [near_ref[k : k + TILE, lanes] for k in range(0, slots, TILE)]
                lows = [index & (LANES - 1) for index in indices]
                highs = [index // LANES for index in indices]
                for b in range(per_device):
                    offsets = []
                    for c in range(3):
                        def own_row(m):
                            at = m // strips * per_device + b
                            return spread_row(
                                own_ref[(*own_lead, slice(at, at + 1), lane_of(m % strips, c))]
                            )
                        sources = [ghost_row(ghost_ref_of, ghost_lead, 0, c, b)]
                        sources += [own_row(m) for m in range(atom_chunks)]
                        sources += [ghost_row(ghost_ref_of, ghost_lead, 1, c, b)]
                        middle = own_row(h * strips + s)
                        offsets.append(
                            [pick(sources, low, high) - middle for low, high in zip(lows, highs)]
                        )
                    totals = [None] * 3
                    for t in range(len(indices)):
                        squared = sum(offsets[c][t] * offsets[c][t] for c in range(3))
                        strength = weight[t * TILE : (t + 1) * TILE, lanes] * jnp.exp(
                            -squared / pair_width
                        )
                        for c in range(3):
                            term = strength * offsets[c][t]
                            totals[c] = term if totals[c] is None else totals[c] + term
                    at = h * per_device + b
                    for c in range(3):
                        total = jnp.sum(totals[c], axis=0, keepdims=True)
                        kick[at : at + 1, lane_of(s, c)] = pair_strength * factor * total
            finish(s)

    def learned(low_high, slot):
        rates = radial_rates(w_in_ref.shape[0])
        for t in range(cover // LANES):
            lanes = pl.ds(pl.multiple_of(first + t * LANES, LANES), LANES)
            indices = [near_ref[k : k + TILE, lanes] for k in range(0, slots, TILE)]
            offsets = []
            for c in range(3):
                low, high = low_high(c)
                own = [spread_row(q_own[c : c + 1, chunk_of(m)]) for m in range(atom_chunks)]
                chunks = [low] + own + [high]
                middle = spread_row(q_own[c : c + 1, lanes])
                offsets.append(
                    [pick(chunks, index & (LANES - 1), index // LANES) - middle for index in indices]
                )
            bases = []
            messages = [None] * len(rates)
            for k in range(len(indices)):
                squared = sum(offsets[c][k] * offsets[c][k] for c in range(3))
                basis = [jnp.exp(-float(rates[r]) * squared) for r in range(2)]
                for r in range(2, len(rates)):
                    basis.append(basis[r - 2] * basis[r - 2])
                bases.append(basis)
                strength = weight[k * TILE : (k + 1) * TILE, lanes]
                for r in range(len(rates)):
                    term = strength * basis[r]
                    messages[r] = term if messages[r] is None else messages[r] + term
            message = jnp.concatenate(
                [jnp.sum(m, axis=0, keepdims=True) for m in messages], axis=0
            ) / slots
            hidden = lax.dot_general(
                w_in_ref[...], message, (((0,), (0,)), ((), ())),
                precision=highest, preferred_element_type=jnp.float32,
            )
            hidden = hidden * jax.nn.sigmoid(hidden)
            radial = dot(w_out_ref[...], hidden)
            spread_radial = [spread_row(radial[r : r + 1, :]) for r in range(len(rates))]
            totals = [None] * 3
            for k in range(len(indices)):
                profile = sum(spread_radial[r] * bases[k][r] for r in range(len(rates)))
                strength = weight[k * TILE : (k + 1) * TILE, lanes] * profile
                for c in range(3):
                    term = strength * offsets[c][k]
                    totals[c] = term if totals[c] is None else totals[c] + term
            tile = jnp.zeros((TILE, LANES), jnp.float32)
            for c in range(3):
                total = spread_row(jnp.sum(totals[c], axis=0, keepdims=True))
                tile = jnp.where(row_at % 4 == c, total, tile)
            tile = jnp.where(row_at // 4 == t % 2, tile, 0.0)
            at = t // 2 * TILE
            if t % 2:
                tile = tile + piece[slot, me, at : at + TILE, :]
            piece[slot, me, at : at + TILE, :] = tile
        start([
            to_peer(piece.at[slot, me], piece.at[slot, me], piece_s.at[slot], piece_r.at[slot], j)
            for j in order
        ])

    def all_pieces(slot, scale):
        line = []
        for s in range(strips):
            for i in range(3):
                tiles = []
                for top in range(0, extra, TILE):
                    tile = jnp.zeros((TILE, LANES), jnp.float32)
                    for row in range(top, min(extra, top + TILE)):
                        h, c = row // CB, row % CB
                        m = h * strips + s
                        source = c * groups + m * LANES // share
                        t = (m * LANES - (source % groups) * share // LANES * LANES) // LANES
                        at = t // 2 * TILE + t % 2 * 4 + i
                        value = piece[slot, source, at : at + 1, :]
                        if scale is not None:
                            value = value * scale[:, chunk_of(m)]
                        tile = jnp.where(row_at == row - top, spread_row(value), tile)
                    tiles.append(tile)
                line.append(jnp.concatenate(tiles, axis=0))
        return jnp.concatenate(line, axis=1)

    def send_kick(step):
        def finish(s):
            lanes = slice(s * wide, (s + 1) * wide)
            if step == 0:
                kicks[0, me, :, lanes] = first_vel[:, lanes] + (0.5 * inner_step) * kick[:, lanes]
            else:
                kick[:, lanes] = inner_step * kick[:, lanes]
                kicks[step, me, :, lanes] = kick[:, lanes]
            start([
                to_peer(kicks.at[step, me, :, lanes], kicks.at[step, me, :, lanes],
                        kick_s.at[step, s], kick_r.at[step, s], j)
                for j in order
            ])
        return finish

    def await_kick(step):
        for s in range(strips):
            lanes = slice(s * wide, (s + 1) * wide)
            for j in order:
                block = kicks.at[step, peers[j], :, lanes]
                to_peer(block, block, kick_s.at[step, s], kick_r.at[step, s], j).wait_recv()

    base_row = extra + TILE
    step_row = [base_row + KINDS * TILE]
    for step in range(NINNER):
        step_row.append(step_row[-1] + (KINDS - step) * TILE)

    cheap(first_pos, (), zg_in, (0,), send_kick(0))
    await_blocks(begin, begin_s, begin_r)
    based = dot(table_ref[base_row : base_row + KINDS * TILE, 0:width], begin[...].reshape(width, -1))
    for copy in qcopies:
        copy.wait_recv()
    learned(lambda c: [spread_row(qg_in[side, c : c + 1, :]) for side in range(2)], 0)
    await_kick(0)
    await_blocks(piece.at[0], piece_s.at[0], piece_r.at[0])
    every = jnp.concatenate((kicks[0].reshape(width, -1), all_pieces(0, inverse)), axis=0)
    based = based + dot(table_ref[step_row[0] : step_row[1], 0 : width + extra], every)
    for kind in range(KINDS):
        acc[kind] = based[kind * TILE : (kind + 1) * TILE, :]

    for side in range(2):
        for t, tile in enumerate(compose(ghost_values(acc, (0,), side, per_device), per_device)):
            zg_out[1, side, t * TILE : (t + 1) * TILE, :] = tile
    ghost_copies = [
        to_side(zg_out.at[1, side], zg_in.at[1, side], zg_s.at[1], zg_r.at[1], side)
        for side in range(2)
    ]
    start(ghost_copies)
    for side in range(2):
        for number, (kind, unit) in enumerate(((1, per_device), (2, per_device), (4, 1))):
            for t, tile in enumerate(compose(ghost_values(acc, (kind,), side, unit), unit)):
                at = (number * ghost_tiles + t) * TILE
                free_out[side, at : at + TILE, :] = tile
    free_copies = [
        to_side(free_out.at[side], free_in.at[side], free_s, free_r, side) for side in range(2)
    ]
    start(free_copies)
    for copy in ghost_copies:
        copy.wait_recv()

    def send_edges(step):
        for side in range(2):
            tiles = compose(ghost_values(kick, (), side, per_device), per_device)
            for t, tile in enumerate(tiles):
                rows = min(TILE, 3 * per_device - t * TILE)
                edge_out[step - 1, side, t * TILE : t * TILE + rows, :] = tile[0:rows]
        start([to_edge(step - 1, side, j, me) for j in order + [0] for side in range(2)])

    def await_edges(step):
        for j in order + [0]:
            for side in range(2):
                to_edge(step - 1, side, j, peers[j]).wait_recv()
        lines = []
        for side in range(2):
            for t in range(ghost_tiles):
                rows = min(TILE, 3 * per_device - t * TILE)
                tiles = []
                for device in range(devices):
                    tile = edge_in[step - 1, side, device, t * TILE : t * TILE + rows, :]
                    if rows < TILE:
                        tile = jnp.concatenate(
                            (tile, jnp.zeros((TILE - rows, LANES), jnp.float32)), axis=0
                        )
                    tiles.append(tile)
                lines.append(jnp.concatenate(tiles, axis=0))
        return jnp.concatenate(lines, axis=1)

    cheap(acc, (0,), zg_in, (1,), send_kick(1))
    send_edges(1)
    for copy in free_copies:
        copy.wait_recv()
    for step in range(1, NINNER):
        await_kick(step)
        table = table_ref[step_row[step] : step_row[step + 1], 0:width]
        moved = dot(table, kicks[step].reshape(width, -1))
        for kind in range(step, KINDS):
            at = (kind - step) * TILE
            acc[kind] = acc[kind] + moved[at : at + TILE, :]
        moved = dot(table, await_edges(step))
        for side in range(2):
            for number, kind in enumerate((1, 2, 4)):
                if kind < step:
                    continue
                at = (kind - step) * TILE
                for t in range(ghost_tiles):
                    line = (side * ghost_tiles + t) * LANES
                    held = (number * ghost_tiles + t) * TILE
                    old = free_in if step == 1 else ghost_acc
                    ghost_acc[side, held : held + TILE, :] = (
                        old[side, held : held + TILE, :] + moved[at : at + TILE, line : line + LANES]
                    )
        if step + 1 == NINNER:
            put_q(lambda i, m: acc[4, m // strips : m // strips + 1, lane_of(m % strips, i)])

            def low_high(c):
                at = (2 * ghost_tiles + c // groups_of) * TILE + c % groups_of
                return [spread_row(ghost_acc[side, at : at + 1, :]) for side in range(2)]

            learned(low_high, 1)
        shifted = ghost_acc.at[:, step_tile(step, ghost_tiles), :]
        if step + 1 < NINNER:
            cheap(acc, (step,), shifted, (), send_kick(step + 1))
            send_edges(step + 1)
        else:
            cheap(acc, (step,), shifted, (), lambda s: None)

    for h in range(halves):
        at = slice(h * per_device, (h + 1) * per_device)
        for s in range(strips):
            for c in range(3):
                new_pos_ref[c, :, chunk_of(h * strips + s)] = acc[2, at, lane_of(s, c)]
    await_blocks(piece.at[1], piece_s.at[1], piece_r.at[1])
    slow = dot(table_ref[extra : extra + TILE, 0:extra], all_pieces(1, None))
    for s in range(strips):
        heavy = mass_rows[:, chunk_of(s)]
        for c in range(3):
            lanes = lane_of(s, c)
            kick[:, lanes] = (
                acc[3, :, lanes] + (0.5 * inner_step) * kick[:, lanes]
            ) * heavy + slow[:, lanes]
    for h in range(halves):
        at = slice(h * per_device, (h + 1) * per_device)
        for s in range(strips):
            for c in range(3):
                new_mom_ref[c, :, chunk_of(h * strips + s)] = kick[at, lane_of(s, c)]
    for copy in sent:
        copy.wait_send()


def step_tile(step, ghost_tiles):
    return slice((step - 1) * ghost_tiles * TILE, step * ghost_tiles * TILE)


def body(
    positions, momenta, neighbours, ghost_rows, species, species_scale, mass_table, w_in, w_out
):
    per_device, _, atoms = positions.shape
    slots = neighbours.shape[0]
    ghosts = ghost_rows.shape[0] // 2
    devices = lax.axis_size("bead")
    table = tables(devices, per_device, atoms)
    groups_of, halves, strips = layout(devices, per_device, atoms)
    ghost_tiles = -(-3 // groups_of)
    extra = halves * CB
    lanes = 3 * LANES * strips
    cover = max(atoms // (devices // CB), LANES)
    lines = -(-3 * (atoms // LANES) // TILE) * TILE
    piece_rows = -(-(cover // LANES) // 2) * TILE
    vmem = pl.BlockSpec(memory_space=pltpu.VMEM)
    hbm = pl.BlockSpec(memory_space=pltpu.HBM)
    f32 = jnp.float32
    dma = pltpu.SemaphoreType.DMA
    operands = (
        positions.transpose(1, 0, 2), momenta.transpose(1, 0, 2), neighbours,
        ghost_rows.reshape(2, ghosts), species.reshape(1, atoms), species_scale.reshape(1, -1),
        mass_table.reshape(1, -1), w_in.T, w_out, table,
    )
    shape = jax.ShapeDtypeStruct(operands[0].shape, f32)
    new_positions, new_momenta = pl.pallas_call(
        cycle_kernel,
        name="cycle",
        out_shape=(shape, shape),
        in_specs=[hbm] * 10,
        out_specs=(vmem, vmem),
        scratch_shapes=[
            pltpu.VMEM((TILE, lanes), f32),
            pltpu.VMEM((TILE, lanes), f32),
            pltpu.VMEM((TILE, strips * LANES), f32),
            pltpu.VMEM((1, atoms), f32),
            pltpu.VMEM((TILE, strips * LANES), f32),
            pltpu.VMEM((slots, atoms), f32),
            pltpu.VMEM((TILE, lanes), f32),
            pltpu.VMEM((KINDS, TILE, lanes), f32),
            pltpu.VMEM((2, 3 * ghost_tiles * TILE, ghosts), f32),
            pltpu.VMEM((devices, TILE, lanes), f32),
            pltpu.VMEM((NINNER, devices, TILE, lanes), f32),
            pltpu.VMEM((2, 2, ghost_tiles * TILE, ghosts), f32),
            pltpu.VMEM((2, 2, ghost_tiles * TILE, ghosts), f32),
            pltpu.VMEM((max(extra, lines), lanes), f32),
            pltpu.VMEM((CB, lines, LANES), f32),
            pltpu.VMEM((devices, lines, LANES), f32),
            pltpu.VMEM((TILE, atoms), f32),
            pltpu.VMEM((2, TILE, ghosts), f32),
            pltpu.VMEM((2, TILE, ghosts), f32),
            pltpu.VMEM((2, devices, piece_rows, LANES), f32),
            pltpu.VMEM((2, 3 * ghost_tiles * TILE, ghosts), f32),
            pltpu.VMEM((2, 3 * ghost_tiles * TILE, ghosts), f32),
            pltpu.VMEM((NINNER - 1, 2, 3 * per_device, ghosts), f32),
            pltpu.VMEM((NINNER - 1, 2, devices, 3 * per_device, ghosts), f32),
            *[pltpu.VMEM(operand.shape, operand.dtype) for operand in operands[:-1]],
            pltpu.VMEM(table.shape[1:], f32),
            dma((len(operands),)),
            dma((2, 2)), dma((2, 2)),
            dma((devices,)), dma((devices,)),
            dma((devices,)), dma((devices,)),
            dma((2,)), dma((2,)),
            dma((NINNER, strips, devices)), dma((NINNER, strips, devices)),
            dma((2, devices)), dma((2, devices)),
            dma((2,)), dma((2,)),
            dma((NINNER - 1, 2, devices)), dma((NINNER - 1, 2, devices)),
        ],
        compiler_params=pltpu.CompilerParams(
            collective_id=0, has_side_effects=True, vmem_limit_bytes=16777216
        ),
    )(*operands)
    return (new_positions.transpose(1, 0, 2), new_momenta.transpose(1, 0, 2))


def solution(mesh):
    in_specs = (
        P("bead", None, "space"),
        P("bead", None, "space"),
        P(None, "space"),
        P("space"),
        P("space"),
        P(),
        P(),
        P(),
        P(),
    )
    out_specs = (P("bead", None, "space"), P("bead", None, "space"))
    return jax.shard_map(body, mesh=mesh, in_specs=in_specs, out_specs=out_specs, check_vma=False)
```

```python
import jax
import jax.numpy as jnp
import numpy as np
from jax import lax
from jax.experimental import pallas as pl
from jax.experimental.pallas import tpu as pltpu
from jax.sharding import PartitionSpec as P

BEADS = 32
CB = 4
NINNER = 3


polymer_freq = 10.0
outer_step = 6.0
pair_width = 1.0
pair_strength = 1.0
highest = lax.Precision.HIGHEST


def mode_matrix(count):
    beadpos = np.arange(count)[None, :]
    modeidx = np.arange(count)[:, None]
    middle = count // 2
    cosine = np.sqrt(2.0 / count) * np.cos(2.0 * np.pi * beadpos * modeidx / count)
    sine_rows = np.sqrt(2.0 / count) * np.sin(2.0 * np.pi * beadpos * modeidx / count)
    matrix = np.where(modeidx < middle, cosine, sine_rows)
    matrix = np.where(modeidx == 0, 1.0 / np.sqrt(count), matrix)
    matrix = np.where(modeidx == middle, np.cos(np.pi * beadpos) / np.sqrt(count), matrix)
    return matrix


def mode_scales(count, inner_step):
    frequency = 2.0 * polymer_freq * np.sin(np.pi * np.arange(count) / count)
    nonzero = np.where(frequency > 0, frequency, 1.0)
    cosine = np.cos(frequency * inner_step)
    drift_gain = np.where(frequency > 0, np.sin(frequency * inner_step) / nonzero, inner_step)
    spring = frequency * np.sin(frequency * inner_step)
    return (cosine, drift_gain, spring)


def contraction(count, fewer):
    full_modes = mode_matrix(count)
    small_modes = mode_matrix(fewer)
    kept = list(range(fewer // 2 + 1)) + list(range(count - fewer // 2 + 1, count))
    contract = np.sqrt(fewer / count) * (small_modes.T @ full_modes[kept])
    expand = count / fewer * contract.T
    return (contract, expand)


def radial_rates(count):
    return 0.2 * 2.0 ** (np.arange(count) / 2.0)

LANES = 128
TILE = 8
KINDS = 5
MESH = pl.DeviceIdType.MESH


def layout(devices, per_device, atoms):
    groups_of = TILE // per_device
    halves = min(atoms // LANES, groups_of)
    return groups_of, halves, atoms // (halves * LANES)


def tables(devices, per_device, atoms):
    inner_step = outer_step / NINNER
    groups_of, halves, _ = layout(devices, per_device, atoms)
    modes = mode_matrix(BEADS)
    contract, expand = contraction(BEADS, CB)
    kick = 0.5 * outer_step * expand

    def power(count):
        cosine, drift_gain, spring = mode_scales(BEADS, inner_step)
        step = np.zeros((2 * BEADS, 2 * BEADS))
        step[:BEADS, :BEADS] = step[BEADS:, BEADS:] = modes.T @ (cosine[:, None] * modes)
        step[:BEADS, BEADS:] = modes.T @ (drift_gain[:, None] * modes)
        step[BEADS:, :BEADS] = -(modes.T @ (spring[:, None] * modes))
        whole = np.linalg.matrix_power(step, count)
        return (whole[:BEADS, :BEADS], whole[:BEADS, BEADS:], whole[BEADS:, :BEADS], whole[BEADS:, BEADS:])

    powers = [power(count) for count in range(NINNER + 1)]
    width = devices * TILE
    extra = halves * CB
    total = -(-(width + extra) // LANES) * LANES
    beads = np.arange(BEADS)
    column = beads // per_device * TILE + beads % per_device

    def block(matrix, device):
        out = np.zeros((TILE, width))
        for q in range(groups_of):
            for b in range(per_device):
                out[q * per_device + b, column + q * per_device] = matrix[device * per_device + b]
        return out

    def member_block(row):
        out = np.zeros((TILE, width))
        for q in range(groups_of):
            out[q, column + q * per_device] = row
        return out

    def piece_block(matrix, device):
        out = np.zeros((TILE, extra))
        for q in range(halves):
            for b in range(per_device):
                out[q * per_device + b, q * CB : (q + 1) * CB] = matrix[device * per_device + b]
        return out

    def piece_member_block(row):
        out = np.zeros((TILE, extra))
        for q in range(halves):
            out[q, q * CB : (q + 1) * CB] = row
        return out

    result = []
    for device in range(devices):
        chosen = contract[device // (devices // CB)]
        rows = []

        def add(left, right=None):
            line = np.zeros((left.shape[0], total))
            line[:, : left.shape[1]] = left
            if right is not None:
                line[:, width : width + extra] = right
            rows.append(line)

        share = np.zeros((CB * halves, TILE))
        for c in range(CB):
            for h in range(halves):
                for b in range(per_device):
                    share[c * halves + h, h * per_device + b] = contract[c, device * per_device + b]
        add(share)
        add(piece_block(kick, device))
        for count in range(1, NINNER + 1):
            add(block(powers[count][0], device))
        add(block(powers[NINNER][2], device))
        add(member_block(chosen @ powers[NINNER][0]))
        for start in range(NINNER):
            for count in range(1, NINNER + 1 - start):
                add(block(powers[count][1], device), piece_block(powers[count][1] @ kick, device))
            last = powers[NINNER - start]
            add(block(last[3], device), piece_block(last[3] @ kick, device))
            add(member_block(chosen @ last[1]), piece_member_block(chosen @ last[1] @ kick))
        result.append(np.concatenate(rows, axis=0))
    return jnp.asarray(np.stack(result), jnp.float32)


def dot(a, b):
    return jnp.dot(a, b, precision=highest, preferred_element_type=jnp.float32)


def lookup(chunk, low):
    return jnp.take_along_axis(chunk, low, axis=1, mode="promise_in_bounds")


def pick(chunks, low, high):
    found = None
    for number, chunk in enumerate(chunks):
        value = lookup(chunk, low)
        found = value if found is None else jnp.where(high == number, value, found)
    return found


def cycle_kernel(
    pos_in, mom_in, near_in, ghost_from, species_in, scale_in, mass_in, w_in_in, w_out_in, table_in,
    new_pos_ref, new_mom_ref,
    first_pos, first_vel, inv_ref, factor_ref, mass_rows, weight, kick, acc, ghost_acc,
    begin, kicks, zg_out, zg_in, part_line, part_out, part_in, q_own, qg_out, qg_in, piece,
    free_out, free_in, edge_out, edge_in, side_out, side_in, side_sum, found_near, found_q,
    inv_row,
    pos_ref, mom_ref, near_ref, ghost_ref, species_ref, scale_ref, mass_ref, w_in_ref, w_out_ref,
    table_ref, load_s, zg_s, zg_r, part_s, part_r, begin_s, begin_r, qg_s, qg_r, kick_s, kick_r,
    piece_s, piece_r, free_s, free_r, edge_s, edge_r, side_s, side_r,
):
    _, per_device, atoms = pos_ref.shape
    slots = near_ref.shape[0]
    ghosts = ghost_ref.shape[1]
    devices = lax.axis_size("bead")
    domains = lax.axis_size("space")
    me = lax.axis_index("bead")
    domain = lax.axis_index("space")
    above = lax.rem(domain + 1, domains)
    below = lax.rem(domain + domains - 1, domains)
    inner_step = outer_step / NINNER
    groups_of, halves, strips = layout(devices, per_device, atoms)
    wide = 3 * LANES
    used = halves * per_device
    ghost_tiles = -(-3 // groups_of)
    groups = devices // CB
    share = atoms // groups
    cover = max(share, LANES)
    member = me // groups
    first = lax.rem(me, groups) * share // LANES * LANES
    atom_chunks = atoms // LANES
    width = devices * TILE
    extra = halves * CB

    def partner(j):
        at, bit = me, 1
        while bit < devices:
            if j & bit:
                at = at + bit - 2 * bit * lax.rem(at // bit, 2)
            bit *= 2
        return at

    peers = [partner(j) for j in range(devices)]
    order = list(range(devices - 1, 0, -1))

    pairs = (
        (pos_in, pos_ref), (mom_in, mom_ref), (species_in, species_ref), (scale_in, scale_ref),
        (mass_in, mass_ref), (ghost_from, ghost_ref), (table_in.at[me], table_ref),
        (near_in, near_ref), (w_in_in, w_in_ref), (w_out_in, w_out_ref),
    )
    loads = [
        pltpu.make_async_copy(src, dst, load_s.at[number])
        for number, (src, dst) in enumerate(pairs)
    ]
    for load in loads:
        load.start()
    barrier = pltpu.get_barrier_semaphore()
    for j in order:
        pl.semaphore_signal(barrier, inc=1, device_id={"bead": peers[j]}, device_id_type=MESH)
    for target in (above, below):
        pl.semaphore_signal(barrier, inc=1, device_id={"space": target}, device_id_type=MESH)

    def to_peer(src, dst, send, recv, j):
        return pltpu.make_async_remote_copy(
            src_ref=src, dst_ref=dst, send_sem=send.at[j], recv_sem=recv.at[j],
            device_id={"bead": peers[j]}, device_id_type=MESH,
        )

    def to_side(src, dst, send, recv, side):
        return pltpu.make_async_remote_copy(
            src_ref=src, dst_ref=dst, send_sem=send.at[side], recv_sem=recv.at[side],
            device_id={"space": (above, below)[side]}, device_id_type=MESH,
        )

    def to_edge(step, side, j, sender):
        return pltpu.make_async_remote_copy(
            src_ref=edge_out.at[step, side], dst_ref=edge_in.at[step, side, sender],
            send_sem=edge_s.at[step, side, j], recv_sem=edge_r.at[step, side, j],
            device_id={"bead": peers[j], "space": (above, below)[side]}, device_id_type=MESH,
        )

    def to_piece_edge(side, j, sender):
        return pltpu.make_async_remote_copy(
            src_ref=side_out.at[side], dst_ref=side_in.at[side, sender],
            send_sem=side_s.at[side, j], recv_sem=side_r.at[side, j],
            device_id={"bead": peers[j], "space": (above, below)[side]}, device_id_type=MESH,
        )

    sent = []

    def start(copies):
        for copy in copies:
            copy.start()
            sent.append(copy)

    def await_blocks(buffer, send, recv):
        for j in order:
            to_peer(buffer.at[peers[j]], buffer.at[peers[j]], send, recv, j).wait_recv()

    row_at = lax.broadcasted_iota(jnp.int32, (TILE, LANES), 0)

    def spread_row(row):
        return jnp.broadcast_to(row, (TILE, LANES))

    def lane_of(strip, c):
        at = (strip * 3 + c) * LANES
        return slice(at, at + LANES)

    def chunk_of(m):
        return slice(m * LANES, (m + 1) * LANES)

    def fold(value, unit):
        shift = unit
        while shift < TILE:
            value = value + pltpu.roll(value, shift, 0)
            shift *= 2
        return value

    def index_of(side):
        index = spread_row(ghost_ref[1 - side : 2 - side, :])
        return index & (LANES - 1), index // LANES

    def ghost_values(ref, lead, side, unit):
        low, high = index_of(side)
        half = high // strips
        strip_at = high - half * strips
        values = []
        for c in range(3):
            parts = [lookup(ref[(*lead, slice(None), lane_of(s, c))], low) for s in range(strips)]
            value = parts[0]
            for s in range(1, strips):
                value = jnp.where(strip_at == s, parts[s], value)
            value = jnp.where(row_at // unit == half, value, 0.0)
            values.append(fold(value, unit))
        return values

    def compose(values, unit):
        tiles = []
        for t in range(ghost_tiles):
            tile = jnp.zeros((TILE, LANES), jnp.float32)
            for c in range(t * groups_of, min(len(values), (t + 1) * groups_of)):
                tile = jnp.where(row_at // unit == c % groups_of, values[c], tile)
            tiles.append(tile)
        return tiles

    for load in loads[:7]:
        load.wait()
    species = species_ref[...]
    charge = jnp.zeros((1, atoms), jnp.float32)
    mass = jnp.zeros((1, atoms), jnp.float32)
    for kind in range(scale_ref.shape[1]):
        charge = jnp.where(species == kind, scale_ref[0:1, kind : kind + 1], charge)
        mass = jnp.where(species == kind, mass_ref[0:1, kind : kind + 1], mass)
    inverse = 1.0 / mass
    factor_ref[...] = charge * inverse
    inv_row[...] = inverse

    if used < TILE:
        first_pos[...] = jnp.zeros(first_pos.shape, jnp.float32)
        first_vel[...] = jnp.zeros(first_vel.shape, jnp.float32)
        kick[...] = jnp.zeros(kick.shape, jnp.float32)
        inv_ref[...] = jnp.zeros(inv_ref.shape, jnp.float32)
        mass_rows[...] = jnp.zeros(mass_rows.shape, jnp.float32)
    for h in range(halves):
        at = slice(h * per_device, (h + 1) * per_device)
        for s in range(strips):
            chunk = chunk_of(h * strips + s)
            for c in range(3):
                first_pos[at, lane_of(s, c)] = pos_ref[c, :, chunk]
    begin[me] = first_pos[...]
    charge_ghosts = []
    for side in range(2):
        low, high = index_of(side)
        parts = [spread_row(charge[:, chunk_of(m)]) for m in range(atom_chunks)]
        values = ghost_values(first_pos, (), side, per_device) + [pick(parts, low, high)]
        for t, tile in enumerate(compose(values, per_device)):
            zg_out[0, side, t * TILE : (t + 1) * TILE, :] = tile

    part_line[0:extra, :] = dot(table_ref[0:extra, 0:TILE], first_pos[...])
    for c in range(CB):
        for i in range(3):
            for m in range(atom_chunks):
                h, s = m // strips, m % strips
                row = c * halves + h
                at = i * atom_chunks + m
                part_out[c, at : at + 1, :] = part_line[row : row + 1, lane_of(s, i)]

    pl.semaphore_wait(barrier, devices + 1)
    ghost_copies = [
        to_side(zg_out.at[0, side], zg_in.at[0, side], zg_s.at[0], zg_r.at[0], side)
        for side in range(2)
    ]
    start(ghost_copies)
    start([to_peer(part_out.at[peers[j] // groups], part_in.at[me], part_s, part_r, j) for j in order])
    start([to_peer(begin.at[me], begin.at[me], begin_s, begin_r, j) for j in order])

    for h in range(halves):
        at = slice(h * per_device, (h + 1) * per_device)
        for s in range(strips):
            chunk = chunk_of(h * strips + s)
            own = jnp.broadcast_to(inverse[:, chunk], (per_device, LANES))
            inv_ref[at, chunk_of(s)] = own
            mass_rows[at, chunk_of(s)] = jnp.broadcast_to(mass[:, chunk], (per_device, LANES))
            for c in range(3):
                first_vel[at, lane_of(s, c)] = mom_ref[c, :, chunk] * own

    def ghost_row(ref, lead, side, c, b):
        at = c // groups_of * TILE + c % groups_of * per_device + b
        return spread_row(ref[(*lead, side, slice(at, at + 1), slice(None))])

    def own_row(ref, lead, m, c, b):
        at = m // strips * per_device + b
        return spread_row(ref[(*lead, slice(at, at + 1), lane_of(m % strips, c))])

    def near_tiles(lanes):
        indices = [near_ref[k : k + TILE, lanes] for k in range(0, slots, TILE)]
        return [index & (LANES - 1) for index in indices], [index // LANES for index in indices]

    def pick_own(sources, low, high):
        found = lookup(sources[0], low)
        for m in range(1, atom_chunks):
            found = jnp.where(high == 1 + m, lookup(sources[m], low), found)
        return found

    def pick_ghost(sides, found, low, high):
        found = jnp.where(high == 0, lookup(sides[0], low), found)
        return jnp.where(high == 1 + atom_chunks, lookup(sides[1], low), found)

    slot_tiles = slots // TILE

    def found_at(m, b, c, t):
        at = (((m * per_device + b) * 3 + c) * slot_tiles + t) * TILE
        return slice(at, at + TILE)

    def cheap_own(own_ref, own_lead):
        for m in range(atom_chunks):
            lows, highs = near_tiles(chunk_of(m))
            for t in range(slot_tiles):
                for b in range(per_device):
                    for c in range(3):
                        sources = [own_row(own_ref, own_lead, k, c, b) for k in range(atom_chunks)]
                        found_near[found_at(m, b, c, t), :] = pick_own(sources, lows[t], highs[t])

    def cheap(own_ref, own_lead, ghost_ref_of, ghost_lead, finish):
        for s in range(strips):
            for h in range(halves):
                m = h * strips + s
                lanes = chunk_of(m)
                factor = factor_ref[:, lanes]
                lows, highs = near_tiles(lanes)
                totals = [[None] * 3 for _ in range(per_device)]
                for t in range(slot_tiles):
                    pull = weight[t * TILE : (t + 1) * TILE, lanes]
                    for b in range(per_device):
                        offsets = []
                        for c in range(3):
                            sides = [
                                ghost_row(ghost_ref_of, ghost_lead, side, c, b) for side in range(2)
                            ]
                            found = found_near[found_at(m, b, c, t), :]
                            offsets.append(
                                pick_ghost(sides, found, lows[t], highs[t])
                                - own_row(own_ref, own_lead, m, c, b)
                            )
                        squared = sum(offset * offset for offset in offsets)
                        strength = pull * jnp.exp(-squared / pair_width)
                        for c in range(3):
                            term = strength * offsets[c]
                            totals[b][c] = term if t == 0 else totals[b][c] + term
                for b in range(per_device):
                    at = h * per_device + b
                    for c in range(3):
                        total = jnp.sum(totals[b][c], axis=0, keepdims=True)
                        kick[at : at + 1, lane_of(s, c)] = pair_strength * factor * total
            finish(s)

    def share_lanes(t):
        return pl.ds(pl.multiple_of(first + t * LANES, LANES), LANES)

    def q_at(t, c, k):
        at = ((t * 3 + c) * slot_tiles + k) * TILE
        return slice(at, at + TILE)

    def learned_own():
        for t in range(cover // LANES):
            lows, highs = near_tiles(share_lanes(t))
            for k in range(slot_tiles):
                for c in range(3):
                    sources = [spread_row(q_own[c : c + 1, chunk_of(m)]) for m in range(atom_chunks)]
                    found_q[q_at(t, c, k), :] = pick_own(sources, lows[k], highs[k])

    def learned(low_high, slot):
        rates = radial_rates(w_in_ref.shape[0])
        forces = []
        for t in range(cover // LANES):
            lanes = share_lanes(t)
            lows, highs = near_tiles(lanes)
            offsets = [[None] * slot_tiles for _ in range(3)]
            for k in range(slot_tiles):
                for c in range(3):
                    found = pick_ghost(low_high(c), found_q[q_at(t, c, k), :], lows[k], highs[k])
                    offsets[c][k] = found - spread_row(q_own[c : c + 1, lanes])
            bases = []
            messages = [None] * len(rates)
            for k in range(slot_tiles):
                squared = sum(offsets[c][k] * offsets[c][k] for c in range(3))
                basis = [jnp.exp(-float(rates[r]) * squared) for r in range(2)]
                for r in range(2, len(rates)):
                    basis.append(basis[r - 2] * basis[r - 2])
                bases.append(basis)
                strength = weight[k * TILE : (k + 1) * TILE, lanes]
                for r in range(len(rates)):
                    term = strength * basis[r]
                    messages[r] = term if messages[r] is None else messages[r] + term
            message = jnp.concatenate(
                [jnp.sum(m, axis=0, keepdims=True) for m in messages], axis=0
            ) / slots
            hidden = lax.dot_general(
                w_in_ref[...], message, (((0,), (0,)), ((), ())),
                precision=highest, preferred_element_type=jnp.float32,
            )
            hidden = hidden * jax.nn.sigmoid(hidden)
            radial = dot(w_out_ref[...], hidden)
            spread_radial = [spread_row(radial[r : r + 1, :]) for r in range(len(rates))]
            totals = [None] * 3
            for k in range(slot_tiles):
                profile = sum(spread_radial[r] * bases[k][r] for r in range(len(rates)))
                strength = weight[k * TILE : (k + 1) * TILE, lanes] * profile
                for c in range(3):
                    term = strength * offsets[c][k]
                    totals[c] = term if totals[c] is None else totals[c] + term
            tile = jnp.zeros((TILE, LANES), jnp.float32)
            for c in range(3):
                total = spread_row(jnp.sum(totals[c], axis=0, keepdims=True))
                tile = jnp.where(row_at % 4 == c, total, tile)
            forces.append(tile)
            tile = jnp.where(row_at // 4 == t % 2, tile, 0.0)
            at = t // 2 * TILE
            if t % 2:
                tile = tile + piece[slot, me, at : at + TILE, :]
            piece[slot, me, at : at + TILE, :] = tile
        if slot == 0:
            begins = lax.rem(me, groups) * share
            for side in range(2):
                index = spread_row(ghost_ref[1 - side : 2 - side, :])
                low, high = index & (LANES - 1), index // LANES
                value = jnp.zeros((TILE, LANES), jnp.float32)
                for t in range(cover // LANES):
                    force = forces[t] * spread_row(inv_row[:, share_lanes(t)])
                    value = jnp.where(high == first // LANES + t, lookup(force, low), value)
                value = jnp.where((index >= begins) & (index < begins + share), value, 0.0)
                side_out[side] = value[0:4]
            start([to_piece_edge(side, j, me) for j in order + [0] for side in range(2)])
        start([
            to_peer(piece.at[slot, me], piece.at[slot, me], piece_s.at[slot], piece_r.at[slot], j)
            for j in order
        ])

    def all_pieces(slot, scale):
        line = []
        for s in range(strips):
            for i in range(3):
                tiles = []
                for top in range(0, extra, TILE):
                    tile = jnp.zeros((TILE, LANES), jnp.float32)
                    for row in range(top, min(extra, top + TILE)):
                        h, c = row // CB, row % CB
                        m = h * strips + s
                        source = c * groups + m * LANES // share
                        t = (m * LANES - (source % groups) * share // LANES * LANES) // LANES
                        at = t // 2 * TILE + t % 2 * 4 + i
                        value = piece[slot, source, at : at + 1, :]
                        if scale is not None:
                            value = value * scale[:, chunk_of(m)]
                        tile = jnp.where(row_at == row - top, spread_row(value), tile)
                    tiles.append(tile)
                line.append(jnp.concatenate(tiles, axis=0))
        return jnp.concatenate(line, axis=1)

    def send_kick(step):
        def finish(s):
            lanes = slice(s * wide, (s + 1) * wide)
            if step == 0:
                kicks[0, me, :, lanes] = first_vel[:, lanes] + (0.5 * inner_step) * kick[:, lanes]
            else:
                kick[:, lanes] = inner_step * kick[:, lanes]
                kicks[step, me, :, lanes] = kick[:, lanes]
            start([
                to_peer(kicks.at[step, me, :, lanes], kicks.at[step, me, :, lanes],
                        kick_s.at[step, s], kick_r.at[step, s], j)
                for j in order
            ])
        return finish

    def await_kick(step):
        for s in range(strips):
            lanes = slice(s * wide, (s + 1) * wide)
            for j in order:
                block = kicks.at[step, peers[j], :, lanes]
                to_peer(block, block, kick_s.at[step, s], kick_r.at[step, s], j).wait_recv()

    base_row = extra + TILE
    step_row = [base_row + KINDS * TILE]
    for step in range(NINNER):
        step_row.append(step_row[-1] + (KINDS - step) * TILE)

    free_kinds = ((0, per_device), (1, per_device), (2, per_device), (4, 1))

    def send_edges(step):
        if step == 0:
            kick[...] = kicks[0, me]
        for side in range(2):
            tiles = compose(ghost_values(kick, (), side, per_device), per_device)
            for t, tile in enumerate(tiles):
                rows = min(TILE, 3 * per_device - t * TILE)
                edge_out[step, side, t * TILE : t * TILE + rows, :] = tile[0:rows]
        start([to_edge(step, side, j, me) for j in order + [0] for side in range(2)])

    def await_edges(step):
        for j in order + [0]:
            for side in range(2):
                to_edge(step, side, j, peers[j]).wait_recv()
        if step == 0:
            for j in order + [0]:
                for side in range(2):
                    to_piece_edge(side, j, peers[j]).wait_recv()
            for side in range(2):
                for c in range(CB):
                    total = side_in[side, c * groups]
                    for part in range(1, groups):
                        total = total + side_in[side, c * groups + part]
                    side_sum[side, c] = total
        lines = []
        for side in range(2):
            for t in range(ghost_tiles):
                rows = min(TILE, 3 * per_device - t * TILE)
                tiles = []
                for device in range(devices):
                    tile = edge_in[step, side, device, t * TILE : t * TILE + rows, :]
                    if rows < TILE:
                        tile = jnp.concatenate(
                            (tile, jnp.zeros((TILE - rows, LANES), jnp.float32)), axis=0
                        )
                    tiles.append(tile)
                if step == 0:
                    for top in range(0, extra, TILE):
                        tile = jnp.zeros((TILE, LANES), jnp.float32)
                        for row in range(top, min(extra, top + TILE)):
                            i, c = t * groups_of + row // CB, row % CB
                            if i < 3:
                                value = spread_row(side_sum[side, c, i : i + 1, :])
                                tile = jnp.where(row_at == row - top, value, tile)
                        tiles.append(tile)
                lines.append(jnp.concatenate(tiles, axis=0))
        return jnp.concatenate(lines, axis=1)

    for load in loads[7:]:
        load.wait()
    cheap_own(first_pos, ())
    await_blocks(part_in, part_s, part_r)
    contracted = part_out[member]
    for j in order:
        contracted = contracted + part_in[peers[j]]
    part_line[0 : contracted.shape[0], 0:LANES] = contracted

    def put_q(value_of):
        for i in range(3):
            for m in range(atom_chunks):
                q_own[i : i + 1, chunk_of(m)] = value_of(i, m)

    put_q(lambda i, m: part_line[i * atom_chunks + m : i * atom_chunks + m + 1, 0:LANES])
    for side in range(2):
        low, high = index_of(side)
        qg_out[side] = pick([q_own[:, chunk_of(m)] for m in range(atom_chunks)], low, high)
    qcopies = [to_side(qg_out.at[side], qg_in.at[side], qg_s, qg_r, side) for side in range(2)]
    start(qcopies)
    learned_own()
    for copy in ghost_copies:
        copy.wait_recv()

    chunks = [ghost_row(zg_in, (0,), 0, 3, 0)]
    chunks += [spread_row(charge[:, chunk_of(m)]) for m in range(atom_chunks)]
    chunks += [ghost_row(zg_in, (0,), 1, 3, 0)]
    for m in range(atom_chunks):
        itself = ghosts + m * LANES + lax.broadcasted_iota(jnp.int32, (TILE, LANES), 1)
        for k in range(0, slots, TILE):
            index = near_ref[k : k + TILE, chunk_of(m)]
            value = pick(chunks, index & (LANES - 1), index // LANES)
            weight[k : k + TILE, chunk_of(m)] = jnp.where(index == itself, 0.0, value)

    cheap(first_pos, (), zg_in, (0,), send_kick(0))
    send_edges(0)
    await_blocks(begin, begin_s, begin_r)
    based = dot(table_ref[base_row : base_row + KINDS * TILE, 0:width], begin[...].reshape(width, -1))
    for kind in range(KINDS):
        acc[kind] = based[kind * TILE : (kind + 1) * TILE, :]
    for side in range(2):
        for number, (kind, unit) in enumerate(free_kinds):
            for t, tile in enumerate(compose(ghost_values(acc, (kind,), side, unit), unit)):
                at = (number * ghost_tiles + t) * TILE
                free_out[side, at : at + TILE, :] = tile
    free_copies = [
        to_side(free_out.at[side], free_in.at[side], free_s, free_r, side) for side in range(2)
    ]
    start(free_copies)
    for copy in qcopies:
        copy.wait_recv()
    learned(lambda c: [spread_row(qg_in[side, c : c + 1, :]) for side in range(2)], 0)
    for copy in free_copies:
        copy.wait_recv()

    for step in range(NINNER):
        last = step + 1 == NINNER
        await_kick(step)
        every = kicks[step].reshape(width, -1)
        depth = width
        if step == 0:
            await_blocks(piece.at[0], piece_s.at[0], piece_r.at[0])
            every = jnp.concatenate((every, all_pieces(0, inverse)), axis=0)
            depth = width + extra
        table = table_ref[step_row[step] : step_row[step + 1], 0:depth]
        moved = dot(table, every)
        for kind in range(step, KINDS):
            at = (kind - step) * TILE
            acc[kind] = acc[kind] + moved[at : at + TILE, :]
        if last:
            put_q(lambda i, m: acc[4, m // strips : m // strips + 1, lane_of(m % strips, i)])
            learned_own()
        cheap_own(acc, (step,))
        moved = dot(table, await_edges(step))
        for side in range(2):
            for number, (kind, _) in enumerate(free_kinds):
                if kind < step:
                    continue
                at = (kind - step) * TILE
                for t in range(ghost_tiles):
                    line = (side * ghost_tiles + t) * LANES
                    held = slice((number * ghost_tiles + t) * TILE, (number * ghost_tiles + t + 1) * TILE)
                    old = free_in if step == 0 else ghost_acc
                    ghost_acc[side, held, :] = (
                        old[side, held, :] + moved[at : at + TILE, line : line + LANES]
                    )
        if last:
            def low_high(c):
                at = (3 * ghost_tiles + c // groups_of) * TILE + c % groups_of
                return [spread_row(ghost_acc[side, at : at + 1, :]) for side in range(2)]

            learned(low_high, 1)
        shifted = ghost_acc.at[:, step * ghost_tiles * TILE : (step + 1) * ghost_tiles * TILE, :]
        if last:
            cheap(acc, (step,), shifted, (), lambda s: None)
        else:
            cheap(acc, (step,), shifted, (), send_kick(step + 1))
            send_edges(step + 1)

    for h in range(halves):
        at = slice(h * per_device, (h + 1) * per_device)
        for s in range(strips):
            for c in range(3):
                new_pos_ref[c, :, chunk_of(h * strips + s)] = acc[2, at, lane_of(s, c)]
    await_blocks(piece.at[1], piece_s.at[1], piece_r.at[1])
    slow = dot(table_ref[extra : extra + TILE, 0:extra], all_pieces(1, None))
    for s in range(strips):
        heavy = mass_rows[:, chunk_of(s)]
        for c in range(3):
            lanes = lane_of(s, c)
            kick[:, lanes] = (
                acc[3, :, lanes] + (0.5 * inner_step) * kick[:, lanes]
            ) * heavy + slow[:, lanes]
    for h in range(halves):
        at = slice(h * per_device, (h + 1) * per_device)
        for s in range(strips):
            for c in range(3):
                new_mom_ref[c, :, chunk_of(h * strips + s)] = kick[at, lane_of(s, c)]
    for copy in sent:
        copy.wait_send()


def body(
    positions, momenta, neighbours, ghost_rows, species, species_scale, mass_table, w_in, w_out
):
    per_device, _, atoms = positions.shape
    slots = neighbours.shape[0]
    ghosts = ghost_rows.shape[0] // 2
    devices = lax.axis_size("bead")
    table = tables(devices, per_device, atoms)
    groups_of, halves, strips = layout(devices, per_device, atoms)
    ghost_tiles = -(-3 // groups_of)
    extra = halves * CB
    lanes = 3 * LANES * strips
    cover = max(atoms // (devices // CB), LANES)
    lines = -(-3 * (atoms // LANES) // TILE) * TILE
    piece_rows = -(-(cover // LANES) // 2) * TILE
    vmem = pl.BlockSpec(memory_space=pltpu.VMEM)
    hbm = pl.BlockSpec(memory_space=pltpu.HBM)
    f32 = jnp.float32
    dma = pltpu.SemaphoreType.DMA
    operands = (
        positions.transpose(1, 0, 2), momenta.transpose(1, 0, 2), neighbours,
        ghost_rows.reshape(2, ghosts), species.reshape(1, atoms), species_scale.reshape(1, -1),
        mass_table.reshape(1, -1), w_in.T, w_out, table,
    )
    shape = jax.ShapeDtypeStruct(operands[0].shape, f32)
    new_positions, new_momenta = pl.pallas_call(
        cycle_kernel,
        name="cycle",
        out_shape=(shape, shape),
        in_specs=[hbm] * 10,
        out_specs=(vmem, vmem),
        scratch_shapes=[
            pltpu.VMEM((TILE, lanes), f32),
            pltpu.VMEM((TILE, lanes), f32),
            pltpu.VMEM((TILE, strips * LANES), f32),
            pltpu.VMEM((1, atoms), f32),
            pltpu.VMEM((TILE, strips * LANES), f32),
            pltpu.VMEM((slots, atoms), f32),
            pltpu.VMEM((TILE, lanes), f32),
            pltpu.VMEM((KINDS, TILE, lanes), f32),
            pltpu.VMEM((2, 4 * ghost_tiles * TILE, ghosts), f32),
            pltpu.VMEM((devices, TILE, lanes), f32),
            pltpu.VMEM((NINNER, devices, TILE, lanes), f32),
            pltpu.VMEM((1, 2, ghost_tiles * TILE, ghosts), f32),
            pltpu.VMEM((1, 2, ghost_tiles * TILE, ghosts), f32),
            pltpu.VMEM((max(extra, lines), lanes), f32),
            pltpu.VMEM((CB, lines, LANES), f32),
            pltpu.VMEM((devices, lines, LANES), f32),
            pltpu.VMEM((TILE, atoms), f32),
            pltpu.VMEM((2, TILE, ghosts), f32),
            pltpu.VMEM((2, TILE, ghosts), f32),
            pltpu.VMEM((2, devices, piece_rows, LANES), f32),
            pltpu.VMEM((2, 4 * ghost_tiles * TILE, ghosts), f32),
            pltpu.VMEM((2, 4 * ghost_tiles * TILE, ghosts), f32),
            pltpu.VMEM((NINNER, 2, 3 * per_device, ghosts), f32),
            pltpu.VMEM((NINNER, 2, devices, 3 * per_device, ghosts), f32),
            pltpu.VMEM((2, 4, ghosts), f32),
            pltpu.VMEM((2, devices, 4, ghosts), f32),
            pltpu.VMEM((2, CB, 4, ghosts), f32),
            pltpu.VMEM((atoms // LANES * per_device * 3 * slots, LANES), f32),
            pltpu.VMEM((cover // LANES * 3 * slots, LANES), f32),
            pltpu.VMEM((1, atoms), f32),
            *[pltpu.VMEM(operand.shape, operand.dtype) for operand in operands[:-1]],
            pltpu.VMEM(table.shape[1:], f32),
            dma((len(operands),)),
            dma((1, 2)), dma((1, 2)),
            dma((devices,)), dma((devices,)),
            dma((devices,)), dma((devices,)),
            dma((2,)), dma((2,)),
            dma((NINNER, strips, devices)), dma((NINNER, strips, devices)),
            dma((2, devices)), dma((2, devices)),
            dma((2,)), dma((2,)),
            dma((NINNER, 2, devices)), dma((NINNER, 2, devices)),
            dma((2, devices)), dma((2, devices)),
        ],
        compiler_params=pltpu.CompilerParams(
            collective_id=0, has_side_effects=True, vmem_limit_bytes=16777216
        ),
    )(*[pltpu.with_memory_space_constraint(x, pltpu.HBM) for x in operands])
    return (new_positions.transpose(1, 0, 2), new_momenta.transpose(1, 0, 2))


def solution(mesh):
    in_specs = (
        P("bead", None, "space"),
        P("bead", None, "space"),
        P(None, "space"),
        P("space"),
        P("space"),
        P(),
        P(),
        P(),
        P(),
    )
    out_specs = (P("bead", None, "space"), P("bead", None, "space"))
    return jax.shard_map(body, mesh=mesh, in_specs=in_specs, out_specs=out_specs, check_vma=False)
```

```python
import jax
import jax.numpy as jnp
import numpy as np
from jax import lax
from jax.experimental import pallas as pl
from jax.experimental.pallas import tpu as pltpu
from jax.sharding import PartitionSpec as P

BEADS = 32
CB = 4
NINNER = 3


polymer_freq = 10.0
outer_step = 6.0
pair_width = 1.0
pair_strength = 1.0
highest = lax.Precision.HIGHEST


def mode_matrix(count):
    beadpos = np.arange(count)[None, :]
    modeidx = np.arange(count)[:, None]
    middle = count // 2
    cosine = np.sqrt(2.0 / count) * np.cos(2.0 * np.pi * beadpos * modeidx / count)
    sine_rows = np.sqrt(2.0 / count) * np.sin(2.0 * np.pi * beadpos * modeidx / count)
    matrix = np.where(modeidx < middle, cosine, sine_rows)
    matrix = np.where(modeidx == 0, 1.0 / np.sqrt(count), matrix)
    matrix = np.where(modeidx == middle, np.cos(np.pi * beadpos) / np.sqrt(count), matrix)
    return matrix


def mode_scales(count, inner_step):
    frequency = 2.0 * polymer_freq * np.sin(np.pi * np.arange(count) / count)
    nonzero = np.where(frequency > 0, frequency, 1.0)
    cosine = np.cos(frequency * inner_step)
    drift_gain = np.where(frequency > 0, np.sin(frequency * inner_step) / nonzero, inner_step)
    spring = frequency * np.sin(frequency * inner_step)
    return (cosine, drift_gain, spring)


def contraction(count, fewer):
    full_modes = mode_matrix(count)
    small_modes = mode_matrix(fewer)
    kept = list(range(fewer // 2 + 1)) + list(range(count - fewer // 2 + 1, count))
    contract = np.sqrt(fewer / count) * (small_modes.T @ full_modes[kept])
    expand = count / fewer * contract.T
    return (contract, expand)


def radial_rates(count):
    return 0.2 * 2.0 ** (np.arange(count) / 2.0)

LANES = 128
TILE = 8
KINDS = 5
MESH = pl.DeviceIdType.MESH


def layout(devices, per_device, atoms):
    groups_of = TILE // per_device
    halves = min(atoms // LANES, groups_of)
    return groups_of, halves, atoms // (halves * LANES)


def tables(devices, per_device, atoms):
    inner_step = outer_step / NINNER
    groups_of, halves, _ = layout(devices, per_device, atoms)
    modes = mode_matrix(BEADS)
    contract, expand = contraction(BEADS, CB)
    kick = 0.5 * outer_step * expand

    def power(count):
        cosine, drift_gain, spring = mode_scales(BEADS, inner_step)
        step = np.zeros((2 * BEADS, 2 * BEADS))
        step[:BEADS, :BEADS] = step[BEADS:, BEADS:] = modes.T @ (cosine[:, None] * modes)
        step[:BEADS, BEADS:] = modes.T @ (drift_gain[:, None] * modes)
        step[BEADS:, :BEADS] = -(modes.T @ (spring[:, None] * modes))
        whole = np.linalg.matrix_power(step, count)
        return (whole[:BEADS, :BEADS], whole[:BEADS, BEADS:], whole[BEADS:, :BEADS], whole[BEADS:, BEADS:])

    powers = [power(count) for count in range(NINNER + 1)]
    width = devices * TILE
    extra = halves * CB
    total = -(-(width + extra) // LANES) * LANES
    beads = np.arange(BEADS)
    column = beads // per_device * TILE + beads % per_device

    def block(matrix, device):
        out = np.zeros((TILE, width))
        for q in range(groups_of):
            for b in range(per_device):
                out[q * per_device + b, column + q * per_device] = matrix[device * per_device + b]
        return out

    def member_block(row):
        out = np.zeros((TILE, width))
        for q in range(groups_of):
            out[q, column + q * per_device] = row
        return out

    def piece_block(matrix, device):
        out = np.zeros((TILE, extra))
        for q in range(halves):
            for b in range(per_device):
                out[q * per_device + b, q * CB : (q + 1) * CB] = matrix[device * per_device + b]
        return out

    def piece_member_block(row):
        out = np.zeros((TILE, extra))
        for q in range(halves):
            out[q, q * CB : (q + 1) * CB] = row
        return out

    result = []
    for device in range(devices):
        chosen = contract[device // (devices // CB)]
        rows = []

        def add(left, right=None):
            line = np.zeros((left.shape[0], total))
            line[:, : left.shape[1]] = left
            if right is not None:
                line[:, width : width + extra] = right
            rows.append(line)

        share = np.zeros((CB * halves, TILE))
        for c in range(CB):
            for h in range(halves):
                for b in range(per_device):
                    share[c * halves + h, h * per_device + b] = contract[c, device * per_device + b]
        add(share)
        add(piece_block(kick, device))
        for count in range(1, NINNER + 1):
            add(block(powers[count][0], device))
        add(block(powers[NINNER][2], device))
        add(member_block(chosen @ powers[NINNER][0]))
        for start in range(NINNER):
            for count in range(1, NINNER + 1 - start):
                add(block(powers[count][1], device), piece_block(powers[count][1] @ kick, device))
            last = powers[NINNER - start]
            add(block(last[3], device), piece_block(last[3] @ kick, device))
            add(member_block(chosen @ last[1]), piece_member_block(chosen @ last[1] @ kick))
        result.append(np.concatenate(rows, axis=0))
    return jnp.asarray(np.stack(result), jnp.float32)


def dot(a, b):
    return jnp.dot(a, b, precision=highest, preferred_element_type=jnp.float32)


def lookup(chunk, low):
    return jnp.take_along_axis(chunk, low, axis=1, mode="promise_in_bounds")


def pick(chunks, low, high):
    found = None
    for number, chunk in enumerate(chunks):
        value = lookup(chunk, low)
        found = value if found is None else jnp.where(high == number, value, found)
    return found


def cycle_kernel(
    pos_in, mom_in, near_in, ghost_from, species_in, scale_in, mass_in, w_in_in, w_out_in, table_in,
    new_ref,
    first_pos, first_vel, inv_ref, factor_ref, mass_rows, weight, kick, acc, ghost_acc,
    begin, kicks, zg_out, zg_in, part_line, part_out, part_in, q_own, qg_out, qg_in, piece,
    free_out, free_in, edge_out, edge_in, side_out, side_in, side_sum, found_near, found_q,
    inv_row,
    pos_ref, mom_ref, near_ref, ghost_ref, species_ref, scale_ref, mass_ref, w_in_ref, w_out_ref,
    table_ref, load_s, send_s, recv_s,
):
    _, per_device, atoms = pos_ref.shape
    slots = near_ref.shape[0]
    ghosts = ghost_ref.shape[1]
    devices = lax.axis_size("bead")
    domains = lax.axis_size("space")
    me = lax.axis_index("bead")
    domain = lax.axis_index("space")
    above = lax.rem(domain + 1, domains)
    below = lax.rem(domain + domains - 1, domains)
    inner_step = outer_step / NINNER
    groups_of, halves, strips = layout(devices, per_device, atoms)
    wide = 3 * LANES
    used = halves * per_device
    ghost_tiles = -(-3 // groups_of)
    groups = devices // CB
    share = atoms // groups
    cover = max(share, LANES)
    member = me // groups
    first = lax.rem(me, groups) * share // LANES * LANES
    atom_chunks = atoms // LANES
    width = devices * TILE
    extra = halves * CB

    def partner(j):
        at, bit = me, 1
        while bit < devices:
            if j & bit:
                at = at + bit - 2 * bit * lax.rem(at // bit, 2)
            bit *= 2
        return at

    peers = [partner(j) for j in range(devices)]
    order = list(range(devices - 1, 0, -1))

    pairs = (
        (pos_in, pos_ref), (mom_in, mom_ref), (species_in, species_ref), (scale_in, scale_ref),
        (mass_in, mass_ref), (ghost_from, ghost_ref), (table_in.at[me], table_ref),
        (near_in, near_ref), (w_in_in, w_in_ref), (w_out_in, w_out_ref),
    )
    loads = [
        pltpu.make_async_copy(src, dst, load_s.at[number])
        for number, (src, dst) in enumerate(pairs)
    ]
    for load in loads:
        load.start()
    barrier = pltpu.get_barrier_semaphore()
    for j in order:
        pl.semaphore_signal(barrier, inc=1, device_id={"bead": peers[j]}, device_id_type=MESH)
    for target in (above, below):
        pl.semaphore_signal(barrier, inc=1, device_id={"space": target}, device_id_type=MESH)

    ghost_at, part_at, begin_at, qghost_at, free_at, side_at = range(6)
    piece_at, kick_at, edge_at = 6, 8, 8 + NINNER
    sent = []

    def remote(src, dst, phase, where):
        return pltpu.make_async_remote_copy(
            src_ref=src, dst_ref=dst, send_sem=send_s.at[phase], recv_sem=recv_s.at[phase],
            device_id=where, device_id_type=MESH,
        )

    def send_peers(src_of, dst, phase):
        for j in order:
            remote(src_of(j), dst, phase, {"bead": peers[j]}).start()

    def send_sides(src, dst, phase):
        for side in range(2):
            remote(src.at[side], dst.at[side], phase, {"space": (above, below)[side]}).start()

    def send_around(src, dst, phase):
        for j in order + [0]:
            for side in range(2):
                where = {"bead": peers[j], "space": (above, below)[side]}
                remote(src.at[side], dst.at[side, me], phase, where).start()

    def arrived(block, phase):
        whole = remote(block, block, phase, {"space": above})
        whole.wait_recv()
        sent.append(whole)

    def others(buffer):
        return buffer.at[0 : devices - 1]

    row_at = lax.broadcasted_iota(jnp.int32, (TILE, LANES), 0)

    def spread_row(row):
        return jnp.broadcast_to(row, (TILE, LANES))

    def lane_of(strip, c):
        at = (strip * 3 + c) * LANES
        return slice(at, at + LANES)

    def chunk_of(m):
        return slice(m * LANES, (m + 1) * LANES)

    def fold(value, unit):
        shift = unit
        while shift < TILE:
            value = value + pltpu.roll(value, shift, 0)
            shift *= 2
        return value

    def index_of(side):
        index = spread_row(ghost_ref[1 - side : 2 - side, :])
        return index & (LANES - 1), index // LANES

    def ghost_values(ref, lead, side, unit):
        low, high = index_of(side)
        half = high // strips
        strip_at = high - half * strips
        values = []
        for c in range(3):
            parts = [lookup(ref[(*lead, slice(None), lane_of(s, c))], low) for s in range(strips)]
            value = parts[0]
            for s in range(1, strips):
                value = jnp.where(strip_at == s, parts[s], value)
            value = jnp.where(row_at // unit == half, value, 0.0)
            values.append(fold(value, unit))
        return values

    def compose(values, unit):
        tiles = []
        for t in range(ghost_tiles):
            tile = jnp.zeros((TILE, LANES), jnp.float32)
            for c in range(t * groups_of, min(len(values), (t + 1) * groups_of)):
                tile = jnp.where(row_at // unit == c % groups_of, values[c], tile)
            tiles.append(tile)
        return tiles

    for load in loads[:7]:
        load.wait()
    species = species_ref[...]
    charge = jnp.zeros((1, atoms), jnp.float32)
    mass = jnp.zeros((1, atoms), jnp.float32)
    for kind in range(scale_ref.shape[1]):
        charge = jnp.where(species == kind, scale_ref[0:1, kind : kind + 1], charge)
        mass = jnp.where(species == kind, mass_ref[0:1, kind : kind + 1], mass)
    inverse = 1.0 / mass
    factor_ref[...] = charge * inverse
    inv_row[...] = inverse

    if used < TILE:
        first_pos[...] = jnp.zeros(first_pos.shape, jnp.float32)
        first_vel[...] = jnp.zeros(first_vel.shape, jnp.float32)
        kick[...] = jnp.zeros(kick.shape, jnp.float32)
        inv_ref[...] = jnp.zeros(inv_ref.shape, jnp.float32)
        mass_rows[...] = jnp.zeros(mass_rows.shape, jnp.float32)
    for h in range(halves):
        at = slice(h * per_device, (h + 1) * per_device)
        for s in range(strips):
            chunk = chunk_of(h * strips + s)
            for c in range(3):
                first_pos[at, lane_of(s, c)] = pos_ref[c, :, chunk]
    begin[me] = first_pos[...]
    charge_ghosts = []
    for side in range(2):
        low, high = index_of(side)
        parts = [spread_row(charge[:, chunk_of(m)]) for m in range(atom_chunks)]
        values = ghost_values(first_pos, (), side, per_device) + [pick(parts, low, high)]
        for t, tile in enumerate(compose(values, per_device)):
            zg_out[side, t * TILE : (t + 1) * TILE, :] = tile

    part_line[0:extra, :] = dot(table_ref[0:extra, 0:TILE], first_pos[...])
    for c in range(CB):
        for i in range(3):
            for m in range(atom_chunks):
                h, s = m // strips, m % strips
                row = c * halves + h
                at = i * atom_chunks + m
                part_out[c, at : at + 1, :] = part_line[row : row + 1, lane_of(s, i)]

    pl.semaphore_wait(barrier, devices + 1)
    send_sides(zg_out, zg_in, ghost_at)
    send_peers(lambda j: part_out.at[peers[j] // groups], part_in.at[me], part_at)
    send_peers(lambda j: begin.at[me], begin.at[me], begin_at)

    for h in range(halves):
        at = slice(h * per_device, (h + 1) * per_device)
        for s in range(strips):
            chunk = chunk_of(h * strips + s)
            own = jnp.broadcast_to(inverse[:, chunk], (per_device, LANES))
            inv_ref[at, chunk_of(s)] = own
            mass_rows[at, chunk_of(s)] = jnp.broadcast_to(mass[:, chunk], (per_device, LANES))
            for c in range(3):
                first_vel[at, lane_of(s, c)] = mom_ref[c, :, chunk] * own

    def ghost_row(ref, lead, side, c, b):
        at = c // groups_of * TILE + c % groups_of * per_device + b
        return spread_row(ref[(*lead, side, slice(at, at + 1), slice(None))])

    def own_row(ref, lead, m, c, b):
        at = m // strips * per_device + b
        return spread_row(ref[(*lead, slice(at, at + 1), lane_of(m % strips, c))])

    def near_tiles(lanes):
        indices = [near_ref[k : k + TILE, lanes] for k in range(0, slots, TILE)]
        return [index & (LANES - 1) for index in indices], [index // LANES for index in indices]

    def pick_own(sources, low, high):
        found = lookup(sources[0], low)
        for m in range(1, atom_chunks):
            found = jnp.where(high == 1 + m, lookup(sources[m], low), found)
        return found

    def pick_ghost(sides, found, low, high):
        found = jnp.where(high == 0, lookup(sides[0], low), found)
        return jnp.where(high == 1 + atom_chunks, lookup(sides[1], low), found)

    slot_tiles = slots // TILE

    def found_at(m, b, c, t):
        at = (((m * per_device + b) * 3 + c) * slot_tiles + t) * TILE
        return slice(at, at + TILE)

    def cheap_own(own_ref, own_lead):
        for m in range(atom_chunks):
            lows, highs = near_tiles(chunk_of(m))
            for t in range(slot_tiles):
                for b in range(per_device):
                    for c in range(3):
                        sources = [own_row(own_ref, own_lead, k, c, b) for k in range(atom_chunks)]
                        found_near[found_at(m, b, c, t), :] = pick_own(sources, lows[t], highs[t])

    def cheap(own_ref, own_lead, ghost_ref_of, ghost_lead, finish):
        for s in range(strips):
            for h in range(halves):
                m = h * strips + s
                lanes = chunk_of(m)
                factor = factor_ref[:, lanes]
                lows, highs = near_tiles(lanes)
                totals = [[None] * 3 for _ in range(per_device)]
                for t in range(slot_tiles):
                    pull = weight[t * TILE : (t + 1) * TILE, lanes]
                    for b in range(per_device):
                        offsets = []
                        for c in range(3):
                            sides = [
                                ghost_row(ghost_ref_of, ghost_lead, side, c, b) for side in range(2)
                            ]
                            found = found_near[found_at(m, b, c, t), :]
                            offsets.append(
                                pick_ghost(sides, found, lows[t], highs[t])
                                - own_row(own_ref, own_lead, m, c, b)
                            )
                        squared = sum(offset * offset for offset in offsets)
                        strength = pull * jnp.exp(-squared / pair_width)
                        for c in range(3):
                            term = strength * offsets[c]
                            totals[b][c] = term if t == 0 else totals[b][c] + term
                for b in range(per_device):
                    at = h * per_device + b
                    for c in range(3):
                        total = jnp.sum(totals[b][c], axis=0, keepdims=True)
                        kick[at : at + 1, lane_of(s, c)] = pair_strength * factor * total
            finish(s)

    def share_lanes(t):
        return pl.ds(pl.multiple_of(first + t * LANES, LANES), LANES)

    def q_at(t, c, k):
        at = ((t * 3 + c) * slot_tiles + k) * TILE
        return slice(at, at + TILE)

    def learned_own():
        for t in range(cover // LANES):
            lows, highs = near_tiles(share_lanes(t))
            for k in range(slot_tiles):
                for c in range(3):
                    sources = [spread_row(q_own[c : c + 1, chunk_of(m)]) for m in range(atom_chunks)]
                    found_q[q_at(t, c, k), :] = pick_own(sources, lows[k], highs[k])

    def learned(low_high, slot):
        rates = radial_rates(w_in_ref.shape[0])
        forces, lines, held = [], [], []
        for t in range(cover // LANES):
            lanes = share_lanes(t)
            lows, highs = near_tiles(lanes)
            offsets = [[None] * slot_tiles for _ in range(3)]
            for k in range(slot_tiles):
                for c in range(3):
                    found = pick_ghost(low_high(c), found_q[q_at(t, c, k), :], lows[k], highs[k])
                    offsets[c][k] = found - spread_row(q_own[c : c + 1, lanes])
            bases = []
            messages = [None] * len(rates)
            for k in range(slot_tiles):
                squared = sum(offsets[c][k] * offsets[c][k] for c in range(3))
                basis = [jnp.exp(-float(rates[r]) * squared) for r in range(2)]
                for r in range(2, len(rates)):
                    basis.append(basis[r - 2] * basis[r - 2])
                bases.append(basis)
                strength = weight[k * TILE : (k + 1) * TILE, lanes]
                for r in range(len(rates)):
                    term = strength * basis[r]
                    messages[r] = term if messages[r] is None else messages[r] + term
            lines.append(jnp.concatenate(
                [jnp.sum(m, axis=0, keepdims=True) for m in messages], axis=0
            ) / slots)
            held.append((offsets, bases))
        hidden = lax.dot_general(
            w_in_ref[...], jnp.concatenate(lines, axis=1), (((0,), (0,)), ((), ())),
            precision=highest, preferred_element_type=jnp.float32,
        )
        hidden = hidden * jax.nn.sigmoid(hidden)
        radials = dot(w_out_ref[...], hidden)
        for t in range(cover // LANES):
            lanes = share_lanes(t)
            offsets, bases = held[t]
            radial = radials[:, t * LANES : (t + 1) * LANES]
            spread_radial = [spread_row(radial[r : r + 1, :]) for r in range(len(rates))]
            totals = [None] * 3
            for k in range(slot_tiles):
                profile = sum(spread_radial[r] * bases[k][r] for r in range(len(rates)))
                strength = weight[k * TILE : (k + 1) * TILE, lanes] * profile
                for c in range(3):
                    term = strength * offsets[c][k]
                    totals[c] = term if totals[c] is None else totals[c] + term
            tile = jnp.zeros((TILE, LANES), jnp.float32)
            for c in range(3):
                total = spread_row(jnp.sum(totals[c], axis=0, keepdims=True))
                tile = jnp.where(row_at % 4 == c, total, tile)
            forces.append(tile)
            tile = jnp.where(row_at // 4 == t % 2, tile, 0.0)
            at = t // 2 * TILE
            if t % 2:
                tile = tile + piece[slot, me, at : at + TILE, :]
            piece[slot, me, at : at + TILE, :] = tile
        if slot == 0:
            begins = lax.rem(me, groups) * share
            for side in range(2):
                index = spread_row(ghost_ref[1 - side : 2 - side, :])
                low, high = index & (LANES - 1), index // LANES
                value = jnp.zeros((TILE, LANES), jnp.float32)
                for t in range(cover // LANES):
                    force = forces[t] * spread_row(inv_row[:, share_lanes(t)])
                    value = jnp.where(high == first // LANES + t, lookup(force, low), value)
                value = jnp.where((index >= begins) & (index < begins + share), value, 0.0)
                side_out[side] = value[0:4]
            send_around(side_out, side_in, side_at)
        send_peers(lambda j: piece.at[slot, me], piece.at[slot, me], piece_at + slot)

    def all_pieces(slot, scale):
        line = []
        for s in range(strips):
            for i in range(3):
                tiles = []
                for top in range(0, extra, TILE):
                    tile = jnp.zeros((TILE, LANES), jnp.float32)
                    for row in range(top, min(extra, top + TILE)):
                        h, c = row // CB, row % CB
                        m = h * strips + s
                        source = c * groups + m * LANES // share
                        t = (m * LANES - (source % groups) * share // LANES * LANES) // LANES
                        at = t // 2 * TILE + t % 2 * 4 + i
                        value = piece[slot, source, at : at + 1, :]
                        if scale is not None:
                            value = value * scale[:, chunk_of(m)]
                        tile = jnp.where(row_at == row - top, spread_row(value), tile)
                    tiles.append(tile)
                line.append(jnp.concatenate(tiles, axis=0))
        return jnp.concatenate(line, axis=1)

    def send_kick(step):
        def finish(s):
            lanes = slice(s * wide, (s + 1) * wide)
            if step == 0:
                kicks[0, me, :, lanes] = first_vel[:, lanes] + (0.5 * inner_step) * kick[:, lanes]
            else:
                kick[:, lanes] = inner_step * kick[:, lanes]
                kicks[step, me, :, lanes] = kick[:, lanes]
            strip = kicks.at[step, me, :, lanes]
            send_peers(lambda j: strip, strip, kick_at + step)
        return finish

    base_row = extra + TILE
    step_row = [base_row + KINDS * TILE]
    for step in range(NINNER):
        step_row.append(step_row[-1] + (KINDS - step) * TILE)

    free_kinds = ((0, per_device), (1, per_device), (2, per_device), (4, 1))

    def send_edges(step):
        if step == 0:
            kick[...] = kicks[0, me]
        for side in range(2):
            tiles = compose(ghost_values(kick, (), side, per_device), per_device)
            for t, tile in enumerate(tiles):
                rows = min(TILE, 3 * per_device - t * TILE)
                edge_out[step, side, t * TILE : t * TILE + rows, :] = tile[0:rows]
        send_around(edge_out.at[step], edge_in.at[step], edge_at + step)

    def await_edges(step):
        arrived(edge_in.at[step], edge_at + step)
        if step == 0:
            arrived(side_in, side_at)
            arrived(free_in, free_at)
            for side in range(2):
                for c in range(CB):
                    total = side_in[side, c * groups]
                    for part in range(1, groups):
                        total = total + side_in[side, c * groups + part]
                    side_sum[side, c] = total
        lines = []
        for side in range(2):
            for t in range(ghost_tiles):
                rows = min(TILE, 3 * per_device - t * TILE)
                tiles = []
                for device in range(devices):
                    tile = edge_in[step, side, device, t * TILE : t * TILE + rows, :]
                    if rows < TILE:
                        tile = jnp.concatenate(
                            (tile, jnp.zeros((TILE - rows, LANES), jnp.float32)), axis=0
                        )
                    tiles.append(tile)
                if step == 0:
                    for top in range(0, extra, TILE):
                        tile = jnp.zeros((TILE, LANES), jnp.float32)
                        for row in range(top, min(extra, top + TILE)):
                            i, c = t * groups_of + row // CB, row % CB
                            if i < 3:
                                value = spread_row(side_sum[side, c, i : i + 1, :])
                                tile = jnp.where(row_at == row - top, value, tile)
                        tiles.append(tile)
                lines.append(jnp.concatenate(tiles, axis=0))
        return jnp.concatenate(lines, axis=1)

    for load in loads[7:]:
        load.wait()
    cheap_own(first_pos, ())
    arrived(others(part_in), part_at)
    contracted = part_out[member]
    for j in order:
        contracted = contracted + part_in[peers[j]]
    part_line[0 : contracted.shape[0], 0:LANES] = contracted

    def put_q(value_of):
        for i in range(3):
            for m in range(atom_chunks):
                q_own[i : i + 1, chunk_of(m)] = value_of(i, m)

    put_q(lambda i, m: part_line[i * atom_chunks + m : i * atom_chunks + m + 1, 0:LANES])
    for side in range(2):
        low, high = index_of(side)
        qg_out[side] = pick([q_own[:, chunk_of(m)] for m in range(atom_chunks)], low, high)
    send_sides(qg_out, qg_in, qghost_at)
    learned_own()
    arrived(zg_in, ghost_at)

    chunks = [ghost_row(zg_in, (), 0, 3, 0)]
    chunks += [spread_row(charge[:, chunk_of(m)]) for m in range(atom_chunks)]
    chunks += [ghost_row(zg_in, (), 1, 3, 0)]
    for m in range(atom_chunks):
        itself = ghosts + m * LANES + lax.broadcasted_iota(jnp.int32, (TILE, LANES), 1)
        for k in range(0, slots, TILE):
            index = near_ref[k : k + TILE, chunk_of(m)]
            value = pick(chunks, index & (LANES - 1), index // LANES)
            weight[k : k + TILE, chunk_of(m)] = jnp.where(index == itself, 0.0, value)

    cheap(first_pos, (), zg_in, (), send_kick(0))
    send_edges(0)
    arrived(others(begin), begin_at)
    based = dot(table_ref[base_row : base_row + KINDS * TILE, 0:width], begin[...].reshape(width, -1))
    for kind in range(KINDS):
        acc[kind] = based[kind * TILE : (kind + 1) * TILE, :]
    for side in range(2):
        for number, (kind, unit) in enumerate(free_kinds):
            for t, tile in enumerate(compose(ghost_values(acc, (kind,), side, unit), unit)):
                at = (number * ghost_tiles + t) * TILE
                free_out[side, at : at + TILE, :] = tile
    send_sides(free_out, free_in, free_at)
    arrived(qg_in, qghost_at)
    learned(lambda c: [spread_row(qg_in[side, c : c + 1, :]) for side in range(2)], 0)

    for step in range(NINNER):
        last = step + 1 == NINNER
        arrived(others(kicks.at[step]), kick_at + step)
        every = kicks[step].reshape(width, -1)
        depth = width
        if step == 0:
            arrived(others(piece.at[0]), piece_at)
            every = jnp.concatenate((every, all_pieces(0, inverse)), axis=0)
            depth = width + extra
        table = table_ref[step_row[step] : step_row[step + 1], 0:depth]
        moved = dot(table, every)
        for kind in range(step, KINDS):
            at = (kind - step) * TILE
            acc[kind] = acc[kind] + moved[at : at + TILE, :]
        if last:
            put_q(lambda i, m: acc[4, m // strips : m // strips + 1, lane_of(m % strips, i)])
            learned_own()
        cheap_own(acc, (step,))
        moved = dot(table, await_edges(step))
        for side in range(2):
            for number, (kind, _) in enumerate(free_kinds):
                if kind < step:
                    continue
                at = (kind - step) * TILE
                for t in range(ghost_tiles):
                    line = (side * ghost_tiles + t) * LANES
                    held = slice((number * ghost_tiles + t) * TILE, (number * ghost_tiles + t + 1) * TILE)
                    old = free_in if step == 0 else ghost_acc
                    ghost_acc[side, held, :] = (
                        old[side, held, :] + moved[at : at + TILE, line : line + LANES]
                    )
        if last:
            def low_high(c):
                at = (3 * ghost_tiles + c // groups_of) * TILE + c % groups_of
                return [spread_row(ghost_acc[side, at : at + 1, :]) for side in range(2)]

            learned(low_high, 1)
        shifted = ghost_acc.at[:, step * ghost_tiles * TILE : (step + 1) * ghost_tiles * TILE, :]
        if last:
            cheap(acc, (step,), shifted, (), lambda s: None)
        else:
            cheap(acc, (step,), shifted, (), send_kick(step + 1))
            send_edges(step + 1)

    for h in range(halves):
        at = slice(h * per_device, (h + 1) * per_device)
        for s in range(strips):
            for c in range(3):
                new_ref[0, c, :, chunk_of(h * strips + s)] = acc[2, at, lane_of(s, c)]
    for copy in sent:
        copy.wait_send()
    arrived(others(piece.at[1]), piece_at + 1)
    slow = dot(table_ref[extra : extra + TILE, 0:extra], all_pieces(1, None))
    for s in range(strips):
        heavy = mass_rows[:, chunk_of(s)]
        for c in range(3):
            lanes = lane_of(s, c)
            kick[:, lanes] = (
                acc[3, :, lanes] + (0.5 * inner_step) * kick[:, lanes]
            ) * heavy + slow[:, lanes]
    for h in range(halves):
        at = slice(h * per_device, (h + 1) * per_device)
        for s in range(strips):
            for c in range(3):
                new_ref[1, c, :, chunk_of(h * strips + s)] = kick[at, lane_of(s, c)]
    sent[-1].wait_send()


def body(
    positions, momenta, neighbours, ghost_rows, species, species_scale, mass_table, w_in, w_out
):
    per_device, _, atoms = positions.shape
    slots = neighbours.shape[0]
    ghosts = ghost_rows.shape[0] // 2
    devices = lax.axis_size("bead")
    table = tables(devices, per_device, atoms)
    groups_of, halves, strips = layout(devices, per_device, atoms)
    ghost_tiles = -(-3 // groups_of)
    extra = halves * CB
    lanes = 3 * LANES * strips
    cover = max(atoms // (devices // CB), LANES)
    lines = -(-3 * (atoms // LANES) // TILE) * TILE
    piece_rows = -(-(cover // LANES) // 2) * TILE
    vmem = pl.BlockSpec(memory_space=pltpu.VMEM)
    hbm = pl.BlockSpec(memory_space=pltpu.HBM)
    f32 = jnp.float32
    dma = pltpu.SemaphoreType.DMA
    operands = (
        positions.transpose(1, 0, 2), momenta.transpose(1, 0, 2), neighbours,
        ghost_rows.reshape(2, ghosts), species.reshape(1, atoms), species_scale.reshape(1, -1),
        mass_table.reshape(1, -1), w_in.T, w_out, table,
    )
    shape = jax.ShapeDtypeStruct((2, *operands[0].shape), f32)
    new = pl.pallas_call(
        cycle_kernel,
        name="cycle",
        out_shape=shape,
        in_specs=[hbm] * 10,
        out_specs=vmem,
        scratch_shapes=[
            pltpu.VMEM((TILE, lanes), f32),
            pltpu.VMEM((TILE, lanes), f32),
            pltpu.VMEM((TILE, strips * LANES), f32),
            pltpu.VMEM((1, atoms), f32),
            pltpu.VMEM((TILE, strips * LANES), f32),
            pltpu.VMEM((slots, atoms), f32),
            pltpu.VMEM((TILE, lanes), f32),
            pltpu.VMEM((KINDS, TILE, lanes), f32),
            pltpu.VMEM((2, 4 * ghost_tiles * TILE, ghosts), f32),
            pltpu.VMEM((devices, TILE, lanes), f32),
            pltpu.VMEM((NINNER, devices, TILE, lanes), f32),
            pltpu.VMEM((2, ghost_tiles * TILE, ghosts), f32),
            pltpu.VMEM((2, ghost_tiles * TILE, ghosts), f32),
            pltpu.VMEM((max(extra, lines), lanes), f32),
            pltpu.VMEM((CB, lines, LANES), f32),
            pltpu.VMEM((devices, lines, LANES), f32),
            pltpu.VMEM((TILE, atoms), f32),
            pltpu.VMEM((2, TILE, ghosts), f32),
            pltpu.VMEM((2, TILE, ghosts), f32),
            pltpu.VMEM((2, devices, piece_rows, LANES), f32),
            pltpu.VMEM((2, 4 * ghost_tiles * TILE, ghosts), f32),
            pltpu.VMEM((2, 4 * ghost_tiles * TILE, ghosts), f32),
            pltpu.VMEM((NINNER, 2, 3 * per_device, ghosts), f32),
            pltpu.VMEM((NINNER, 2, devices, 3 * per_device, ghosts), f32),
            pltpu.VMEM((2, 4, ghosts), f32),
            pltpu.VMEM((2, devices, 4, ghosts), f32),
            pltpu.VMEM((2, CB, 4, ghosts), f32),
            pltpu.VMEM((atoms // LANES * per_device * 3 * slots, LANES), f32),
            pltpu.VMEM((cover // LANES * 3 * slots, LANES), f32),
            pltpu.VMEM((1, atoms), f32),
            *[pltpu.VMEM(operand.shape, operand.dtype) for operand in operands[:-1]],
            pltpu.VMEM(table.shape[1:], f32),
            dma((len(operands),)),
            dma((8 + 2 * NINNER,)), dma((8 + 2 * NINNER,)),
        ],
        compiler_params=pltpu.CompilerParams(
            collective_id=0, has_side_effects=True, vmem_limit_bytes=16777216
        ),
    )(*[pltpu.with_memory_space_constraint(x, pltpu.HBM) for x in operands])
    return (new[0].transpose(1, 0, 2), new[1].transpose(1, 0, 2))


def solution(mesh):
    in_specs = (
        P("bead", None, "space"),
        P("bead", None, "space"),
        P(None, "space"),
        P("space"),
        P("space"),
        P(),
        P(),
        P(),
        P(),
    )
    out_specs = (P("bead", None, "space"), P("bead", None, "space"))
    return jax.shard_map(body, mesh=mesh, in_specs=in_specs, out_specs=out_specs, check_vma=False)
```

```python
import jax
import jax.numpy as jnp
import numpy as np
from jax import lax
from jax.experimental import pallas as pl
from jax.experimental.pallas import tpu as pltpu
from jax.sharding import PartitionSpec as P

BEADS = 32
CB = 4
NINNER = 3


polymer_freq = 10.0
outer_step = 6.0
pair_width = 1.0
pair_strength = 1.0
highest = lax.Precision.HIGHEST


def mode_matrix(count):
    beadpos = np.arange(count)[None, :]
    modeidx = np.arange(count)[:, None]
    middle = count // 2
    cosine = np.sqrt(2.0 / count) * np.cos(2.0 * np.pi * beadpos * modeidx / count)
    sine_rows = np.sqrt(2.0 / count) * np.sin(2.0 * np.pi * beadpos * modeidx / count)
    matrix = np.where(modeidx < middle, cosine, sine_rows)
    matrix = np.where(modeidx == 0, 1.0 / np.sqrt(count), matrix)
    matrix = np.where(modeidx == middle, np.cos(np.pi * beadpos) / np.sqrt(count), matrix)
    return matrix


def mode_scales(count, inner_step):
    frequency = 2.0 * polymer_freq * np.sin(np.pi * np.arange(count) / count)
    nonzero = np.where(frequency > 0, frequency, 1.0)
    cosine = np.cos(frequency * inner_step)
    drift_gain = np.where(frequency > 0, np.sin(frequency * inner_step) / nonzero, inner_step)
    spring = frequency * np.sin(frequency * inner_step)
    return (cosine, drift_gain, spring)


def contraction(count, fewer):
    full_modes = mode_matrix(count)
    small_modes = mode_matrix(fewer)
    kept = list(range(fewer // 2 + 1)) + list(range(count - fewer // 2 + 1, count))
    contract = np.sqrt(fewer / count) * (small_modes.T @ full_modes[kept])
    expand = count / fewer * contract.T
    return (contract, expand)


def radial_rates(count):
    return 0.2 * 2.0 ** (np.arange(count) / 2.0)

LANES = 128
TILE = 8
KINDS = 5
MESH = pl.DeviceIdType.MESH


def layout(devices, per_device, atoms):
    groups_of = TILE // per_device
    halves = min(atoms // LANES, groups_of)
    return groups_of, halves, atoms // (halves * LANES)


def tables(devices, per_device, atoms):
    inner_step = outer_step / NINNER
    groups_of, halves, _ = layout(devices, per_device, atoms)
    modes = mode_matrix(BEADS)
    contract, expand = contraction(BEADS, CB)
    kick = 0.5 * outer_step * expand

    def power(count):
        cosine, drift_gain, spring = mode_scales(BEADS, inner_step)
        step = np.zeros((2 * BEADS, 2 * BEADS))
        step[:BEADS, :BEADS] = step[BEADS:, BEADS:] = modes.T @ (cosine[:, None] * modes)
        step[:BEADS, BEADS:] = modes.T @ (drift_gain[:, None] * modes)
        step[BEADS:, :BEADS] = -(modes.T @ (spring[:, None] * modes))
        whole = np.linalg.matrix_power(step, count)
        return (whole[:BEADS, :BEADS], whole[:BEADS, BEADS:], whole[BEADS:, :BEADS], whole[BEADS:, BEADS:])

    powers = [power(count) for count in range(NINNER + 1)]
    width = devices * TILE
    extra = halves * CB
    total = -(-(width + extra) // LANES) * LANES
    beads = np.arange(BEADS)
    column = beads // per_device * TILE + beads % per_device

    def block(matrix, device):
        out = np.zeros((TILE, width))
        for q in range(groups_of):
            for b in range(per_device):
                out[q * per_device + b, column + q * per_device] = matrix[device * per_device + b]
        return out

    def member_block(row):
        out = np.zeros((TILE, width))
        for q in range(groups_of):
            out[q, column + q * per_device] = row
        return out

    def piece_block(matrix, device):
        out = np.zeros((TILE, extra))
        for q in range(halves):
            for b in range(per_device):
                out[q * per_device + b, q * CB : (q + 1) * CB] = matrix[device * per_device + b]
        return out

    def piece_member_block(row):
        out = np.zeros((TILE, extra))
        for q in range(halves):
            out[q, q * CB : (q + 1) * CB] = row
        return out

    result = []
    for device in range(devices):
        chosen = contract[device // (devices // CB)]
        rows = []

        def add(left, right=None):
            line = np.zeros((left.shape[0], total))
            line[:, : left.shape[1]] = left
            if right is not None:
                line[:, width : width + extra] = right
            rows.append(line)

        share = np.zeros((CB * halves, TILE))
        for c in range(CB):
            for h in range(halves):
                for b in range(per_device):
                    share[c * halves + h, h * per_device + b] = contract[c, device * per_device + b]
        add(share)
        add(piece_block(kick, device))
        for count in range(1, NINNER + 1):
            add(block(powers[count][0], device))
        add(block(powers[NINNER][2], device))
        add(member_block(chosen @ powers[NINNER][0]))
        for start in range(NINNER):
            for count in range(1, NINNER + 1 - start):
                add(block(powers[count][1], device), piece_block(powers[count][1] @ kick, device))
            last = powers[NINNER - start]
            add(block(last[3], device), piece_block(last[3] @ kick, device))
            add(member_block(chosen @ last[1]), piece_member_block(chosen @ last[1] @ kick))
        result.append(np.concatenate(rows, axis=0))
    return jnp.asarray(np.stack(result), jnp.float32)


def dot(a, b):
    return jnp.dot(a, b, precision=highest, preferred_element_type=jnp.float32)


def lookup(chunk, low):
    return jnp.take_along_axis(chunk, low, axis=1, mode="promise_in_bounds")


def pick(chunks, low, high):
    found = None
    for number, chunk in enumerate(chunks):
        value = lookup(chunk, low)
        found = value if found is None else jnp.where(high == number, value, found)
    return found


def cycle_kernel(
    pos_in, mom_in, near_in, ghost_from, species_in, scale_in, mass_in, w_in_in, w_out_in, table_in,
    new_ref,
    first_pos, first_vel, inv_ref, factor_ref, mass_rows, weight, kick, acc, ghost_acc,
    begin, kicks, zg_out, zg_in, part_line, part_out, part_in, q_own, qg_out, qg_in, piece,
    free_out, free_in, edge_out, edge_in, side_out, side_in, side_sum, found_near, found_q,
    inv_row,
    pos_ref, mom_ref, near_ref, ghost_ref, species_ref, scale_ref, mass_ref, w_in_ref, w_out_ref,
    table_ref, load_s, send_s, recv_s,
):
    _, per_device, atoms = pos_ref.shape
    slots = near_ref.shape[0]
    ghosts = ghost_ref.shape[1]
    devices = lax.axis_size("bead")
    domains = lax.axis_size("space")
    me = lax.axis_index("bead")
    domain = lax.axis_index("space")
    above = lax.rem(domain + 1, domains)
    below = lax.rem(domain + domains - 1, domains)
    inner_step = outer_step / NINNER
    groups_of, halves, strips = layout(devices, per_device, atoms)
    wide = 3 * LANES
    used = halves * per_device
    ghost_tiles = -(-3 // groups_of)
    groups = devices // CB
    share = atoms // groups
    cover = max(share, LANES)
    member = me // groups
    first = lax.rem(me, groups) * share // LANES * LANES
    atom_chunks = atoms // LANES
    width = devices * TILE
    extra = halves * CB

    def partner(j):
        at, bit = me, 1
        while bit < devices:
            if j & bit:
                at = at + bit - 2 * bit * lax.rem(at // bit, 2)
            bit *= 2
        return at

    peers = [partner(j) for j in range(devices)]
    order = list(range(devices - 1, 0, -1))

    pairs = (
        (pos_in, pos_ref), (mom_in, mom_ref), (species_in, species_ref), (scale_in, scale_ref),
        (mass_in, mass_ref), (ghost_from, ghost_ref), (table_in.at[me], table_ref),
        (near_in, near_ref), (w_in_in, w_in_ref), (w_out_in, w_out_ref),
    )
    loads = [
        pltpu.make_async_copy(src, dst, load_s.at[number])
        for number, (src, dst) in enumerate(pairs)
    ]
    for load in loads:
        load.start()
    barrier = pltpu.get_barrier_semaphore()
    for j in order:
        pl.semaphore_signal(barrier, inc=1, device_id={"bead": peers[j]}, device_id_type=MESH)
    for target in (above, below):
        pl.semaphore_signal(barrier, inc=1, device_id={"space": target}, device_id_type=MESH)

    ghost_at, part_at, begin_at, qghost_at, free_at, side_at = range(6)
    piece_at, kick_at, edge_at = 6, 8, 8 + NINNER
    sent = []

    def remote(src, dst, phase, where):
        return pltpu.make_async_remote_copy(
            src_ref=src, dst_ref=dst, send_sem=send_s.at[phase], recv_sem=recv_s.at[phase],
            device_id=where, device_id_type=MESH,
        )

    def send_peers(src_of, dst, phase):
        for j in order:
            remote(src_of(j), dst, phase, {"bead": peers[j]}).start()

    def send_sides(src, dst, phase):
        for side in range(2):
            remote(src.at[side], dst.at[side], phase, {"space": (above, below)[side]}).start()

    def send_around(src, dst, phase):
        for j in order + [0]:
            for side in range(2):
                where = {"bead": peers[j], "space": (above, below)[side]}
                remote(src.at[side], dst.at[side, me], phase, where).start()

    def arrived(block, phase):
        whole = remote(block, block, phase, {"space": above})
        whole.wait_recv()
        sent.append(whole)

    def others(buffer):
        return buffer.at[0 : devices - 1]

    row_at = lax.broadcasted_iota(jnp.int32, (TILE, LANES), 0)

    def spread_row(row):
        return jnp.broadcast_to(row, (TILE, LANES))

    def lane_of(strip, c):
        at = (strip * 3 + c) * LANES
        return slice(at, at + LANES)

    def chunk_of(m):
        return slice(m * LANES, (m + 1) * LANES)

    def fold(value, unit):
        shift = unit
        while shift < TILE:
            value = value + pltpu.roll(value, shift, 0)
            shift *= 2
        return value

    def index_of(side):
        index = spread_row(ghost_ref[1 - side : 2 - side, :])
        return index & (LANES - 1), index // LANES

    def ghost_values(ref, lead, side, unit):
        low, high = index_of(side)
        half = high // strips
        strip_at = high - half * strips
        values = []
        for c in range(3):
            parts = [lookup(ref[(*lead, slice(None), lane_of(s, c))], low) for s in range(strips)]
            value = parts[0]
            for s in range(1, strips):
                value = jnp.where(strip_at == s, parts[s], value)
            value = jnp.where(row_at // unit == half, value, 0.0)
            values.append(fold(value, unit))
        return values

    def compose(values, unit):
        tiles = []
        for t in range(ghost_tiles):
            tile = jnp.zeros((TILE, LANES), jnp.float32)
            for c in range(t * groups_of, min(len(values), (t + 1) * groups_of)):
                tile = jnp.where(row_at // unit == c % groups_of, values[c], tile)
            tiles.append(tile)
        return tiles

    for load in loads[:7]:
        load.wait()
    species = species_ref[...]
    charge = jnp.zeros((1, atoms), jnp.float32)
    mass = jnp.zeros((1, atoms), jnp.float32)
    for kind in range(scale_ref.shape[1]):
        charge = jnp.where(species == kind, scale_ref[0:1, kind : kind + 1], charge)
        mass = jnp.where(species == kind, mass_ref[0:1, kind : kind + 1], mass)
    inverse = 1.0 / mass
    factor_ref[...] = charge * inverse
    inv_row[...] = inverse

    if used < TILE:
        first_pos[...] = jnp.zeros(first_pos.shape, jnp.float32)
        first_vel[...] = jnp.zeros(first_vel.shape, jnp.float32)
        kick[...] = jnp.zeros(kick.shape, jnp.float32)
        inv_ref[...] = jnp.zeros(inv_ref.shape, jnp.float32)
        mass_rows[...] = jnp.zeros(mass_rows.shape, jnp.float32)
    for h in range(halves):
        at = slice(h * per_device, (h + 1) * per_device)
        for s in range(strips):
            chunk = chunk_of(h * strips + s)
            for c in range(3):
                first_pos[at, lane_of(s, c)] = pos_ref[c, :, chunk]
    begin[me] = first_pos[...]
    charge_ghosts = []
    for side in range(2):
        low, high = index_of(side)
        parts = [spread_row(charge[:, chunk_of(m)]) for m in range(atom_chunks)]
        values = ghost_values(first_pos, (), side, per_device) + [pick(parts, low, high)]
        for t, tile in enumerate(compose(values, per_device)):
            zg_out[side, t * TILE : (t + 1) * TILE, :] = tile

    part_line[0:extra, :] = dot(table_ref[0:extra, 0:TILE], first_pos[...])
    for c in range(CB):
        for i in range(3):
            for m in range(atom_chunks):
                h, s = m // strips, m % strips
                row = c * halves + h
                at = i * atom_chunks + m
                part_out[c, at : at + 1, :] = part_line[row : row + 1, lane_of(s, i)]

    pl.semaphore_wait(barrier, devices + 1)
    send_sides(zg_out, zg_in, ghost_at)
    send_peers(lambda j: part_out.at[peers[j] // groups], part_in.at[me], part_at)
    send_peers(lambda j: begin.at[me], begin.at[me], begin_at)

    for h in range(halves):
        at = slice(h * per_device, (h + 1) * per_device)
        for s in range(strips):
            chunk = chunk_of(h * strips + s)
            own = jnp.broadcast_to(inverse[:, chunk], (per_device, LANES))
            inv_ref[at, chunk_of(s)] = own
            mass_rows[at, chunk_of(s)] = jnp.broadcast_to(mass[:, chunk], (per_device, LANES))
            for c in range(3):
                first_vel[at, lane_of(s, c)] = mom_ref[c, :, chunk] * own

    def ghost_row(ref, lead, side, c, b):
        at = c // groups_of * TILE + c % groups_of * per_device + b
        return spread_row(ref[(*lead, side, slice(at, at + 1), slice(None))])

    def own_row(ref, lead, m, c, b):
        at = m // strips * per_device + b
        return spread_row(ref[(*lead, slice(at, at + 1), lane_of(m % strips, c))])

    def near_tiles(lanes):
        indices = [near_ref[k : k + TILE, lanes] for k in range(0, slots, TILE)]
        return [index & (LANES - 1) for index in indices], [index // LANES for index in indices]

    def pick_own(sources, low, high):
        found = lookup(sources[0], low)
        for m in range(1, atom_chunks):
            found = jnp.where(high == 1 + m, lookup(sources[m], low), found)
        return found

    def pick_ghost(sides, found, low, high):
        found = jnp.where(high == 0, lookup(sides[0], low), found)
        return jnp.where(high == 1 + atom_chunks, lookup(sides[1], low), found)

    slot_tiles = slots // TILE

    def found_at(m, b, c, t):
        at = (((m * per_device + b) * 3 + c) * slot_tiles + t) * TILE
        return slice(at, at + TILE)

    def cheap_own(own_ref, own_lead):
        for m in range(atom_chunks):
            lows, highs = near_tiles(chunk_of(m))
            for t in range(slot_tiles):
                for b in range(per_device):
                    for c in range(3):
                        sources = [own_row(own_ref, own_lead, k, c, b) for k in range(atom_chunks)]
                        found_near[found_at(m, b, c, t), :] = pick_own(sources, lows[t], highs[t])

    def cheap(own_ref, own_lead, ghost_ref_of, ghost_lead, finish):
        for s in range(strips):
            for h in range(halves):
                m = h * strips + s
                lanes = chunk_of(m)
                factor = factor_ref[:, lanes]
                lows, highs = near_tiles(lanes)
                totals = [[None] * 3 for _ in range(per_device)]
                for t in range(slot_tiles):
                    pull = weight[t * TILE : (t + 1) * TILE, lanes]
                    for b in range(per_device):
                        offsets = []
                        for c in range(3):
                            sides = [
                                ghost_row(ghost_ref_of, ghost_lead, side, c, b) for side in range(2)
                            ]
                            found = found_near[found_at(m, b, c, t), :]
                            offsets.append(
                                pick_ghost(sides, found, lows[t], highs[t])
                                - own_row(own_ref, own_lead, m, c, b)
                            )
                        squared = sum(offset * offset for offset in offsets)
                        strength = pull * jnp.exp(-squared / pair_width)
                        for c in range(3):
                            term = strength * offsets[c]
                            totals[b][c] = term if t == 0 else totals[b][c] + term
                for b in range(per_device):
                    at = h * per_device + b
                    for c in range(3):
                        total = jnp.sum(totals[b][c], axis=0, keepdims=True)
                        kick[at : at + 1, lane_of(s, c)] = pair_strength * factor * total
            finish(s)

    def share_lanes(t):
        return pl.ds(pl.multiple_of(first + t * LANES, LANES), LANES)

    def q_at(t, c, k):
        at = ((t * 3 + c) * slot_tiles + k) * TILE
        return slice(at, at + TILE)

    def learned_own():
        for t in range(cover // LANES):
            lows, highs = near_tiles(share_lanes(t))
            for k in range(slot_tiles):
                for c in range(3):
                    sources = [spread_row(q_own[c : c + 1, chunk_of(m)]) for m in range(atom_chunks)]
                    found_q[q_at(t, c, k), :] = pick_own(sources, lows[k], highs[k])

    def learned(low_high, slot):
        rates = radial_rates(w_in_ref.shape[0])
        forces, lines, held = [], [], []
        for t in range(cover // LANES):
            lanes = share_lanes(t)
            lows, highs = near_tiles(lanes)
            offsets = [[None] * slot_tiles for _ in range(3)]
            for k in range(slot_tiles):
                for c in range(3):
                    found = pick_ghost(low_high(c), found_q[q_at(t, c, k), :], lows[k], highs[k])
                    offsets[c][k] = found - spread_row(q_own[c : c + 1, lanes])
            bases = []
            messages = [None] * len(rates)
            for k in range(slot_tiles):
                squared = sum(offsets[c][k] * offsets[c][k] for c in range(3))
                basis = [jnp.exp(-float(rates[r]) * squared) for r in range(2)]
                for r in range(2, len(rates)):
                    basis.append(basis[r - 2] * basis[r - 2])
                bases.append(basis)
                strength = weight[k * TILE : (k + 1) * TILE, lanes]
                for r in range(len(rates)):
                    term = strength * basis[r]
                    messages[r] = term if messages[r] is None else messages[r] + term
            lines.append(jnp.concatenate(
                [jnp.sum(m, axis=0, keepdims=True) for m in messages], axis=0
            ) / slots)
            held.append((offsets, bases))
        hidden = lax.dot_general(
            w_in_ref[...], jnp.concatenate(lines, axis=1), (((0,), (0,)), ((), ())),
            precision=highest, preferred_element_type=jnp.float32,
        )
        hidden = hidden * jax.nn.sigmoid(hidden)
        radials = dot(w_out_ref[...], hidden)
        for t in range(cover // LANES):
            lanes = share_lanes(t)
            offsets, bases = held[t]
            radial = radials[:, t * LANES : (t + 1) * LANES]
            spread_radial = [spread_row(radial[r : r + 1, :]) for r in range(len(rates))]
            totals = [None] * 3
            for k in range(slot_tiles):
                profile = sum(spread_radial[r] * bases[k][r] for r in range(len(rates)))
                strength = weight[k * TILE : (k + 1) * TILE, lanes] * profile
                for c in range(3):
                    term = strength * offsets[c][k]
                    totals[c] = term if totals[c] is None else totals[c] + term
            tile = jnp.zeros((TILE, LANES), jnp.float32)
            for c in range(3):
                total = spread_row(jnp.sum(totals[c], axis=0, keepdims=True))
                tile = jnp.where(row_at % 4 == c, total, tile)
            forces.append(tile)
            tile = jnp.where(row_at // 4 == t % 2, tile, 0.0)
            at = t // 2 * TILE
            if t % 2:
                tile = tile + piece[slot, me, at : at + TILE, :]
            piece[slot, me, at : at + TILE, :] = tile
        if slot == 0:
            begins = lax.rem(me, groups) * share
            for side in range(2):
                index = spread_row(ghost_ref[1 - side : 2 - side, :])
                low, high = index & (LANES - 1), index // LANES
                value = jnp.zeros((TILE, LANES), jnp.float32)
                for t in range(cover // LANES):
                    force = forces[t] * spread_row(inv_row[:, share_lanes(t)])
                    value = jnp.where(high == first // LANES + t, lookup(force, low), value)
                value = jnp.where((index >= begins) & (index < begins + share), value, 0.0)
                side_out[side] = value[0:4]
            send_around(side_out, side_in, side_at)
        send_peers(lambda j: piece.at[slot, me], piece.at[slot, me], piece_at + slot)

    def all_pieces(slot, scale):
        line = []
        for s in range(strips):
            for i in range(3):
                tiles = []
                for top in range(0, extra, TILE):
                    tile = jnp.zeros((TILE, LANES), jnp.float32)
                    for row in range(top, min(extra, top + TILE)):
                        h, c = row // CB, row % CB
                        m = h * strips + s
                        source = c * groups + m * LANES // share
                        t = (m * LANES - (source % groups) * share // LANES * LANES) // LANES
                        at = t // 2 * TILE + t % 2 * 4 + i
                        value = piece[slot, source, at : at + 1, :]
                        if scale is not None:
                            value = value * scale[:, chunk_of(m)]
                        tile = jnp.where(row_at == row - top, spread_row(value), tile)
                    tiles.append(tile)
                line.append(jnp.concatenate(tiles, axis=0))
        return jnp.concatenate(line, axis=1)

    def send_kick(step):
        def finish(s):
            lanes = slice(s * wide, (s + 1) * wide)
            if step == 0:
                kicks[0, me, :, lanes] = first_vel[:, lanes] + (0.5 * inner_step) * kick[:, lanes]
            else:
                kick[:, lanes] = inner_step * kick[:, lanes]
                kicks[step, me, :, lanes] = kick[:, lanes]
            strip = kicks.at[step, me, :, lanes]
            send_peers(lambda j: strip, strip, kick_at + step)
        return finish

    base_row = extra + TILE
    step_row = [base_row + KINDS * TILE]
    for step in range(NINNER):
        step_row.append(step_row[-1] + (KINDS - step) * TILE)

    free_kinds = ((0, per_device), (1, per_device), (2, per_device), (4, 1))

    def send_edges(step):
        if step == 0:
            kick[...] = kicks[0, me]
        for side in range(2):
            tiles = compose(ghost_values(kick, (), side, per_device), per_device)
            for t, tile in enumerate(tiles):
                rows = min(TILE, 3 * per_device - t * TILE)
                edge_out[step, side, t * TILE : t * TILE + rows, :] = tile[0:rows]
        send_around(edge_out.at[step], edge_in.at[step], edge_at + step)

    def await_edges(step):
        arrived(edge_in.at[step], edge_at + step)
        if step == 0:
            arrived(side_in, side_at)
            arrived(free_in, free_at)
            for side in range(2):
                for c in range(CB):
                    total = side_in[side, c * groups]
                    for part in range(1, groups):
                        total = total + side_in[side, c * groups + part]
                    side_sum[side, c] = total
        lines = []
        for side in range(2):
            for t in range(ghost_tiles):
                rows = min(TILE, 3 * per_device - t * TILE)
                tiles = []
                for device in range(devices):
                    tile = edge_in[step, side, device, t * TILE : t * TILE + rows, :]
                    if rows < TILE:
                        tile = jnp.concatenate(
                            (tile, jnp.zeros((TILE - rows, LANES), jnp.float32)), axis=0
                        )
                    tiles.append(tile)
                if step == 0:
                    for top in range(0, extra, TILE):
                        tile = jnp.zeros((TILE, LANES), jnp.float32)
                        for row in range(top, min(extra, top + TILE)):
                            i, c = t * groups_of + row // CB, row % CB
                            if i < 3:
                                value = spread_row(side_sum[side, c, i : i + 1, :])
                                tile = jnp.where(row_at == row - top, value, tile)
                        tiles.append(tile)
                lines.append(jnp.concatenate(tiles, axis=0))
        return jnp.concatenate(lines, axis=1)

    for load in loads[7:]:
        load.wait()
    cheap_own(first_pos, ())
    arrived(others(part_in), part_at)
    contracted = part_out[member]
    for j in order:
        contracted = contracted + part_in[peers[j]]
    part_line[0 : contracted.shape[0], 0:LANES] = contracted

    def put_q(value_of):
        for i in range(3):
            for m in range(atom_chunks):
                q_own[i : i + 1, chunk_of(m)] = value_of(i, m)

    put_q(lambda i, m: part_line[i * atom_chunks + m : i * atom_chunks + m + 1, 0:LANES])
    for side in range(2):
        low, high = index_of(side)
        qg_out[side] = pick([q_own[:, chunk_of(m)] for m in range(atom_chunks)], low, high)[0:4]
    send_sides(qg_out, qg_in, qghost_at)
    learned_own()
    arrived(zg_in, ghost_at)

    chunks = [ghost_row(zg_in, (), 0, 3, 0)]
    chunks += [spread_row(charge[:, chunk_of(m)]) for m in range(atom_chunks)]
    chunks += [ghost_row(zg_in, (), 1, 3, 0)]
    for m in range(atom_chunks):
        itself = ghosts + m * LANES + lax.broadcasted_iota(jnp.int32, (TILE, LANES), 1)
        for k in range(0, slots, TILE):
            index = near_ref[k : k + TILE, chunk_of(m)]
            value = pick(chunks, index & (LANES - 1), index // LANES)
            weight[k : k + TILE, chunk_of(m)] = jnp.where(index == itself, 0.0, value)

    cheap(first_pos, (), zg_in, (), send_kick(0))
    send_edges(0)
    arrived(others(begin), begin_at)
    based = dot(table_ref[base_row : base_row + KINDS * TILE, 0:width], begin[...].reshape(width, -1))
    for kind in range(KINDS):
        acc[kind] = based[kind * TILE : (kind + 1) * TILE, :]
    for side in range(2):
        for number, (kind, unit) in enumerate(free_kinds):
            for t, tile in enumerate(compose(ghost_values(acc, (kind,), side, unit), unit)):
                at = (number * ghost_tiles + t) * TILE
                free_out[side, at : at + TILE, :] = tile
    send_sides(free_out, free_in, free_at)
    arrived(qg_in, qghost_at)
    learned(lambda c: [spread_row(qg_in[side, c : c + 1, :]) for side in range(2)], 0)

    for step in range(NINNER):
        last = step + 1 == NINNER
        arrived(others(kicks.at[step]), kick_at + step)
        every = kicks[step].reshape(width, -1)
        depth = width
        if step == 0:
            arrived(others(piece.at[0]), piece_at)
            every = jnp.concatenate((every, all_pieces(0, inverse)), axis=0)
            depth = width + extra
        table = table_ref[step_row[step] : step_row[step + 1], 0:depth]
        moved = dot(table, every)
        for kind in range(step, KINDS):
            at = (kind - step) * TILE
            acc[kind] = acc[kind] + moved[at : at + TILE, :]
        if last:
            put_q(lambda i, m: acc[4, m // strips : m // strips + 1, lane_of(m % strips, i)])
            learned_own()
        else:
            cheap_own(acc, (step,))
        moved = dot(table, await_edges(step))
        for side in range(2):
            for number, (kind, _) in enumerate(free_kinds):
                if kind < step:
                    continue
                at = (kind - step) * TILE
                for t in range(ghost_tiles):
                    line = (side * ghost_tiles + t) * LANES
                    held = slice((number * ghost_tiles + t) * TILE, (number * ghost_tiles + t + 1) * TILE)
                    old = free_in if step == 0 else ghost_acc
                    ghost_acc[side, held, :] = (
                        old[side, held, :] + moved[at : at + TILE, line : line + LANES]
                    )
        if last:
            def low_high(c):
                at = (3 * ghost_tiles + c // groups_of) * TILE + c % groups_of
                return [spread_row(ghost_acc[side, at : at + 1, :]) for side in range(2)]

            learned(low_high, 1)
        shifted = ghost_acc.at[:, step * ghost_tiles * TILE : (step + 1) * ghost_tiles * TILE, :]
        if last:
            cheap_own(acc, (step,))
            cheap(acc, (step,), shifted, (), lambda s: None)
        else:
            cheap(acc, (step,), shifted, (), send_kick(step + 1))
            send_edges(step + 1)

    for h in range(halves):
        at = slice(h * per_device, (h + 1) * per_device)
        for s in range(strips):
            for c in range(3):
                new_ref[0, c, :, chunk_of(h * strips + s)] = acc[2, at, lane_of(s, c)]
    for copy in sent:
        copy.wait_send()
    arrived(others(piece.at[1]), piece_at + 1)
    slow = dot(table_ref[extra : extra + TILE, 0:extra], all_pieces(1, None))
    for s in range(strips):
        heavy = mass_rows[:, chunk_of(s)]
        for c in range(3):
            lanes = lane_of(s, c)
            kick[:, lanes] = (
                acc[3, :, lanes] + (0.5 * inner_step) * kick[:, lanes]
            ) * heavy + slow[:, lanes]
    for h in range(halves):
        at = slice(h * per_device, (h + 1) * per_device)
        for s in range(strips):
            for c in range(3):
                new_ref[1, c, :, chunk_of(h * strips + s)] = kick[at, lane_of(s, c)]
    sent[-1].wait_send()


def body(
    positions, momenta, neighbours, ghost_rows, species, species_scale, mass_table, w_in, w_out
):
    per_device, _, atoms = positions.shape
    slots = neighbours.shape[0]
    ghosts = ghost_rows.shape[0] // 2
    devices = lax.axis_size("bead")
    table = tables(devices, per_device, atoms)
    groups_of, halves, strips = layout(devices, per_device, atoms)
    ghost_tiles = -(-3 // groups_of)
    extra = halves * CB
    lanes = 3 * LANES * strips
    cover = max(atoms // (devices // CB), LANES)
    lines = 3 * (atoms // LANES)
    piece_rows = -(-(cover // LANES) // 2) * TILE
    vmem = pl.BlockSpec(memory_space=pltpu.VMEM)
    hbm = pl.BlockSpec(memory_space=pltpu.HBM)
    f32 = jnp.float32
    dma = pltpu.SemaphoreType.DMA
    operands = (
        positions.transpose(1, 0, 2), momenta.transpose(1, 0, 2), neighbours,
        ghost_rows.reshape(2, ghosts), species.reshape(1, atoms), species_scale.reshape(1, -1),
        mass_table.reshape(1, -1), w_in.T, w_out, table,
    )
    shape = jax.ShapeDtypeStruct((2, *operands[0].shape), f32)
    new = pl.pallas_call(
        cycle_kernel,
        name="cycle",
        out_shape=shape,
        in_specs=[hbm] * 10,
        out_specs=vmem,
        scratch_shapes=[
            pltpu.VMEM((TILE, lanes), f32),
            pltpu.VMEM((TILE, lanes), f32),
            pltpu.VMEM((TILE, strips * LANES), f32),
            pltpu.VMEM((1, atoms), f32),
            pltpu.VMEM((TILE, strips * LANES), f32),
            pltpu.VMEM((slots, atoms), f32),
            pltpu.VMEM((TILE, lanes), f32),
            pltpu.VMEM((KINDS, TILE, lanes), f32),
            pltpu.VMEM((2, 4 * ghost_tiles * TILE, ghosts), f32),
            pltpu.VMEM((devices, TILE, lanes), f32),
            pltpu.VMEM((NINNER, devices, TILE, lanes), f32),
            pltpu.VMEM((2, ghost_tiles * TILE, ghosts), f32),
            pltpu.VMEM((2, ghost_tiles * TILE, ghosts), f32),
            pltpu.VMEM((max(extra, -(-lines // TILE) * TILE), lanes), f32),
            pltpu.VMEM((CB, lines, LANES), f32),
            pltpu.VMEM((devices, lines, LANES), f32),
            pltpu.VMEM((TILE, atoms), f32),
            pltpu.VMEM((2, 4, ghosts), f32),
            pltpu.VMEM((2, 4, ghosts), f32),
            pltpu.VMEM((2, devices, piece_rows, LANES), f32),
            pltpu.VMEM((2, 4 * ghost_tiles * TILE, ghosts), f32),
            pltpu.VMEM((2, 4 * ghost_tiles * TILE, ghosts), f32),
            pltpu.VMEM((NINNER, 2, 3 * per_device, ghosts), f32),
            pltpu.VMEM((NINNER, 2, devices, 3 * per_device, ghosts), f32),
            pltpu.VMEM((2, 4, ghosts), f32),
            pltpu.VMEM((2, devices, 4, ghosts), f32),
            pltpu.VMEM((2, CB, 4, ghosts), f32),
            pltpu.VMEM((atoms // LANES * per_device * 3 * slots, LANES), f32),
            pltpu.VMEM((cover // LANES * 3 * slots, LANES), f32),
            pltpu.VMEM((1, atoms), f32),
            *[pltpu.VMEM(operand.shape, operand.dtype) for operand in operands[:-1]],
            pltpu.VMEM(table.shape[1:], f32),
            dma((len(operands),)),
            dma((8 + 2 * NINNER,)), dma((8 + 2 * NINNER,)),
        ],
        compiler_params=pltpu.CompilerParams(
            collective_id=0, has_side_effects=True, vmem_limit_bytes=16777216
        ),
    )(*[pltpu.with_memory_space_constraint(x, pltpu.HBM) for x in operands])
    return (new[0].transpose(1, 0, 2), new[1].transpose(1, 0, 2))


def solution(mesh):
    in_specs = (
        P("bead", None, "space"),
        P("bead", None, "space"),
        P(None, "space"),
        P("space"),
        P("space"),
        P(),
        P(),
        P(),
        P(),
    )
    out_specs = (P("bead", None, "space"), P("bead", None, "space"))
    return jax.shard_map(body, mesh=mesh, in_specs=in_specs, out_specs=out_specs, check_vma=False)
```

```python
import jax
import jax.numpy as jnp
import numpy as np
from jax import lax
from jax.experimental import pallas as pl
from jax.experimental.pallas import tpu as pltpu
from jax.sharding import PartitionSpec as P

BEADS = 32
CB = 4
NINNER = 3


polymer_freq = 10.0
outer_step = 6.0
pair_width = 1.0
pair_strength = 1.0
highest = lax.Precision.HIGHEST


def mode_matrix(count):
    beadpos = np.arange(count)[None, :]
    modeidx = np.arange(count)[:, None]
    middle = count // 2
    cosine = np.sqrt(2.0 / count) * np.cos(2.0 * np.pi * beadpos * modeidx / count)
    sine_rows = np.sqrt(2.0 / count) * np.sin(2.0 * np.pi * beadpos * modeidx / count)
    matrix = np.where(modeidx < middle, cosine, sine_rows)
    matrix = np.where(modeidx == 0, 1.0 / np.sqrt(count), matrix)
    matrix = np.where(modeidx == middle, np.cos(np.pi * beadpos) / np.sqrt(count), matrix)
    return matrix


def mode_scales(count, inner_step):
    frequency = 2.0 * polymer_freq * np.sin(np.pi * np.arange(count) / count)
    nonzero = np.where(frequency > 0, frequency, 1.0)
    cosine = np.cos(frequency * inner_step)
    drift_gain = np.where(frequency > 0, np.sin(frequency * inner_step) / nonzero, inner_step)
    spring = frequency * np.sin(frequency * inner_step)
    return (cosine, drift_gain, spring)


def contraction(count, fewer):
    full_modes = mode_matrix(count)
    small_modes = mode_matrix(fewer)
    kept = list(range(fewer // 2 + 1)) + list(range(count - fewer // 2 + 1, count))
    contract = np.sqrt(fewer / count) * (small_modes.T @ full_modes[kept])
    expand = count / fewer * contract.T
    return (contract, expand)


def radial_rates(count):
    return 0.2 * 2.0 ** (np.arange(count) / 2.0)

LANES = 128
TILE = 8
KINDS = 5
MESH = pl.DeviceIdType.MESH


def layout(devices, per_device, atoms):
    groups_of = TILE // per_device
    halves = min(atoms // LANES, groups_of)
    return groups_of, halves, atoms // (halves * LANES)


def tables(devices, per_device, atoms):
    inner_step = outer_step / NINNER
    groups_of, halves, _ = layout(devices, per_device, atoms)
    modes = mode_matrix(BEADS)
    contract, expand = contraction(BEADS, CB)
    kick = 0.5 * outer_step * expand

    def power(count):
        cosine, drift_gain, spring = mode_scales(BEADS, inner_step)
        step = np.zeros((2 * BEADS, 2 * BEADS))
        step[:BEADS, :BEADS] = step[BEADS:, BEADS:] = modes.T @ (cosine[:, None] * modes)
        step[:BEADS, BEADS:] = modes.T @ (drift_gain[:, None] * modes)
        step[BEADS:, :BEADS] = -(modes.T @ (spring[:, None] * modes))
        whole = np.linalg.matrix_power(step, count)
        return (whole[:BEADS, :BEADS], whole[:BEADS, BEADS:], whole[BEADS:, :BEADS], whole[BEADS:, BEADS:])

    powers = [power(count) for count in range(NINNER + 1)]
    width = devices * TILE
    extra = halves * CB
    total = -(-(width + extra) // LANES) * LANES
    beads = np.arange(BEADS)
    column = beads // per_device * TILE + beads % per_device

    def block(matrix, device):
        out = np.zeros((TILE, width))
        for q in range(groups_of):
            for b in range(per_device):
                out[q * per_device + b, column + q * per_device] = matrix[device * per_device + b]
        return out

    def member_block(row):
        out = np.zeros((TILE, width))
        for q in range(groups_of):
            out[q, column + q * per_device] = row
        return out

    def piece_block(matrix, device):
        out = np.zeros((TILE, extra))
        for q in range(halves):
            for b in range(per_device):
                out[q * per_device + b, q * CB : (q + 1) * CB] = matrix[device * per_device + b]
        return out

    def piece_member_block(row):
        out = np.zeros((TILE, extra))
        for q in range(halves):
            out[q, q * CB : (q + 1) * CB] = row
        return out

    result = []
    for device in range(devices):
        chosen = contract[device // (devices // CB)]
        rows = []

        def add(left, right=None):
            line = np.zeros((left.shape[0], total))
            line[:, : left.shape[1]] = left
            if right is not None:
                line[:, width : width + extra] = right
            rows.append(line)

        share = np.zeros((CB * halves, TILE))
        for c in range(CB):
            for h in range(halves):
                for b in range(per_device):
                    share[c * halves + h, h * per_device + b] = contract[c, device * per_device + b]
        add(share)
        add(piece_block(kick, device))
        for count in range(1, NINNER + 1):
            add(block(powers[count][0], device))
        add(block(powers[NINNER][2], device))
        add(member_block(chosen @ powers[NINNER][0]))
        for start in range(NINNER):
            for count in range(1, NINNER + 1 - start):
                add(block(powers[count][1], device), piece_block(powers[count][1] @ kick, device))
            last = powers[NINNER - start]
            add(block(last[3], device), piece_block(last[3] @ kick, device))
            add(member_block(chosen @ last[1]), piece_member_block(chosen @ last[1] @ kick))
        result.append(np.concatenate(rows, axis=0))
    return jnp.asarray(np.stack(result), jnp.float32)


def dot(a, b):
    return jnp.dot(a, b, precision=highest, preferred_element_type=jnp.float32)


def lookup(chunk, low):
    return jnp.take_along_axis(chunk, low, axis=1, mode="promise_in_bounds")


def pick(chunks, low, high):
    found = None
    for number, chunk in enumerate(chunks):
        value = lookup(chunk, low)
        found = value if found is None else jnp.where(high == number, value, found)
    return found


def cycle_kernel(
    pos_in, mom_in, near_in, ghost_from, species_in, scale_in, mass_in, w_in_in, w_out_in, table_in,
    new_ref,
    first_pos, first_vel, inv_ref, factor_ref, mass_rows, weight, kick, acc, ghost_acc,
    begin, kicks, zg_out, zg_in, part_line, part_out, part_in, q_own, qg_out, qg_in, piece,
    free_out, free_in, edge_out, edge_in, side_out, side_in, side_sum, found_near, found_q,
    inv_row,
    pos_ref, mom_ref, near_ref, ghost_ref, species_ref, scale_ref, mass_ref, w_in_ref, w_out_ref,
    table_ref, load_s, send_s, recv_s,
):
    _, per_device, atoms = pos_ref.shape
    slots = near_ref.shape[0]
    ghosts = ghost_ref.shape[1]
    devices = lax.axis_size("bead")
    domains = lax.axis_size("space")
    me = lax.axis_index("bead")
    domain = lax.axis_index("space")
    above = lax.rem(domain + 1, domains)
    below = lax.rem(domain + domains - 1, domains)
    inner_step = outer_step / NINNER
    groups_of, halves, strips = layout(devices, per_device, atoms)
    wide = 3 * LANES
    used = halves * per_device
    ghost_tiles = -(-3 // groups_of)
    groups = devices // CB
    share = atoms // groups
    cover = max(share, LANES)
    member = me // groups
    first = lax.rem(me, groups) * share // LANES * LANES
    atom_chunks = atoms // LANES
    width = devices * TILE
    extra = halves * CB

    steps = {}
    bit = 1
    while bit < devices:
        steps[bit] = bit - 2 * bit * lax.rem(lax.div(me, bit), 2)
        bit *= 2

    def partner(j):
        return sum((steps[bit] for bit in steps if j & bit), me)

    peers = [partner(j) for j in range(devices)]
    order = list(range(devices - 1, 0, -1))

    pairs = (
        (pos_in, pos_ref), (mom_in, mom_ref), (species_in, species_ref), (scale_in, scale_ref),
        (mass_in, mass_ref), (ghost_from, ghost_ref), (table_in.at[me], table_ref),
        (near_in, near_ref), (w_in_in, w_in_ref), (w_out_in, w_out_ref),
    )
    loads = [
        pltpu.make_async_copy(src, dst, load_s.at[number])
        for number, (src, dst) in enumerate(pairs)
    ]
    barrier = pltpu.get_barrier_semaphore()
    for target in (above, below):
        pl.semaphore_signal(barrier, inc=1, device_id={"space": target}, device_id_type=MESH)
    for j in order:
        pl.semaphore_signal(barrier, inc=1, device_id={"bead": peers[j]}, device_id_type=MESH)
    for load in loads:
        load.start()

    ghost_at, part_at, begin_at, qghost_at, free_at, side_at = range(6)
    piece_at, kick_at, edge_at = 6, 8, 8 + NINNER
    sent = []

    def remote(src, dst, phase, where):
        return pltpu.make_async_remote_copy(
            src_ref=src, dst_ref=dst, send_sem=send_s.at[phase], recv_sem=recv_s.at[phase],
            device_id=where, device_id_type=MESH,
        )

    def send_peers(src_of, dst, phase):
        for j in order:
            remote(src_of(j), dst, phase, {"bead": peers[j]}).start()

    def send_sides(src, dst, phase):
        for side in range(2):
            remote(src.at[side], dst.at[side], phase, {"space": (above, below)[side]}).start()

    def send_around(src, dst, phase):
        for j in order + [0]:
            for side in range(2):
                where = {"bead": peers[j], "space": (above, below)[side]}
                remote(src.at[side], dst.at[side, me], phase, where).start()

    def arrived(block, phase):
        whole = remote(block, block, phase, {"space": above})
        whole.wait_recv()
        sent.append(whole)

    def others(buffer):
        return buffer.at[0 : devices - 1]

    row_at = lax.broadcasted_iota(jnp.int32, (TILE, LANES), 0)

    def spread_row(row):
        return jnp.broadcast_to(row, (TILE, LANES))

    def lane_of(strip, c):
        at = (strip * 3 + c) * LANES
        return slice(at, at + LANES)

    def chunk_of(m):
        return slice(m * LANES, (m + 1) * LANES)

    def fold(value, unit):
        shift = unit
        while shift < TILE:
            value = value + pltpu.roll(value, shift, 0)
            shift *= 2
        return value

    def index_of(side):
        index = spread_row(ghost_ref[1 - side : 2 - side, :])
        return index & (LANES - 1), index // LANES

    def ghost_values(ref, lead, side, unit):
        low, high = index_of(side)
        half = high // strips
        strip_at = high - half * strips
        values = []
        for c in range(3):
            parts = [lookup(ref[(*lead, slice(None), lane_of(s, c))], low) for s in range(strips)]
            value = parts[0]
            for s in range(1, strips):
                value = jnp.where(strip_at == s, parts[s], value)
            value = jnp.where(row_at // unit == half, value, 0.0)
            values.append(fold(value, unit))
        return values

    def compose(values, unit):
        tiles = []
        for t in range(ghost_tiles):
            tile = jnp.zeros((TILE, LANES), jnp.float32)
            for c in range(t * groups_of, min(len(values), (t + 1) * groups_of)):
                tile = jnp.where(row_at // unit == c % groups_of, values[c], tile)
            tiles.append(tile)
        return tiles

    for load in loads[:7]:
        load.wait()
    species = species_ref[...]
    charge = jnp.zeros((1, atoms), jnp.float32)
    mass = jnp.zeros((1, atoms), jnp.float32)
    for kind in range(scale_ref.shape[1]):
        charge = jnp.where(species == kind, scale_ref[0:1, kind : kind + 1], charge)
        mass = jnp.where(species == kind, mass_ref[0:1, kind : kind + 1], mass)
    inverse = 1.0 / mass
    factor_ref[...] = charge * inverse
    inv_row[...] = inverse

    if used < TILE:
        first_pos[...] = jnp.zeros(first_pos.shape, jnp.float32)
        first_vel[...] = jnp.zeros(first_vel.shape, jnp.float32)
        kick[...] = jnp.zeros(kick.shape, jnp.float32)
        inv_ref[...] = jnp.zeros(inv_ref.shape, jnp.float32)
        mass_rows[...] = jnp.zeros(mass_rows.shape, jnp.float32)
    for h in range(halves):
        at = slice(h * per_device, (h + 1) * per_device)
        for s in range(strips):
            chunk = chunk_of(h * strips + s)
            for c in range(3):
                first_pos[at, lane_of(s, c)] = pos_ref[c, :, chunk]
    begin[me] = first_pos[...]
    charge_ghosts = []
    for side in range(2):
        low, high = index_of(side)
        parts = [spread_row(charge[:, chunk_of(m)]) for m in range(atom_chunks)]
        values = ghost_values(first_pos, (), side, per_device) + [pick(parts, low, high)]
        for t, tile in enumerate(compose(values, per_device)):
            zg_out[side, t * TILE : (t + 1) * TILE, :] = tile

    part_line[0:extra, :] = dot(table_ref[0:extra, 0:TILE], first_pos[...])
    for c in range(CB):
        for i in range(3):
            for m in range(atom_chunks):
                h, s = m // strips, m % strips
                row = c * halves + h
                at = i * atom_chunks + m
                part_out[c, at : at + 1, :] = part_line[row : row + 1, lane_of(s, i)]

    pl.semaphore_wait(barrier, devices + 1)
    send_peers(lambda j: part_out.at[lax.div(peers[j], groups)], part_in.at[me], part_at)
    send_sides(zg_out, zg_in, ghost_at)
    send_peers(lambda j: begin.at[me], begin.at[me], begin_at)

    for h in range(halves):
        at = slice(h * per_device, (h + 1) * per_device)
        for s in range(strips):
            chunk = chunk_of(h * strips + s)
            own = jnp.broadcast_to(inverse[:, chunk], (per_device, LANES))
            inv_ref[at, chunk_of(s)] = own
            mass_rows[at, chunk_of(s)] = jnp.broadcast_to(mass[:, chunk], (per_device, LANES))
            for c in range(3):
                first_vel[at, lane_of(s, c)] = mom_ref[c, :, chunk] * own

    def ghost_row(ref, lead, side, c, b):
        at = c // groups_of * TILE + c % groups_of * per_device + b
        return spread_row(ref[(*lead, side, slice(at, at + 1), slice(None))])

    def own_row(ref, lead, m, c, b):
        at = m // strips * per_device + b
        return spread_row(ref[(*lead, slice(at, at + 1), lane_of(m % strips, c))])

    def near_tiles(lanes):
        indices = [near_ref[k : k + TILE, lanes] for k in range(0, slots, TILE)]
        return [index & (LANES - 1) for index in indices], [index // LANES for index in indices]

    def pick_own(sources, low, high):
        found = lookup(sources[0], low)
        for m in range(1, atom_chunks):
            found = jnp.where(high == 1 + m, lookup(sources[m], low), found)
        return found

    def pick_ghost(sides, found, low, high):
        found = jnp.where(high == 0, lookup(sides[0], low), found)
        return jnp.where(high == 1 + atom_chunks, lookup(sides[1], low), found)

    slot_tiles = slots // TILE

    def found_at(m, b, c, t):
        at = (((m * per_device + b) * 3 + c) * slot_tiles + t) * TILE
        return slice(at, at + TILE)

    def cheap_own(own_ref, own_lead):
        for m in range(atom_chunks):
            lows, highs = near_tiles(chunk_of(m))
            for t in range(slot_tiles):
                for b in range(per_device):
                    for c in range(3):
                        sources = [own_row(own_ref, own_lead, k, c, b) for k in range(atom_chunks)]
                        found_near[found_at(m, b, c, t), :] = pick_own(sources, lows[t], highs[t])

    def cheap(own_ref, own_lead, ghost_ref_of, ghost_lead, finish):
        for s in range(strips):
            for h in range(halves):
                m = h * strips + s
                lanes = chunk_of(m)
                factor = factor_ref[:, lanes]
                lows, highs = near_tiles(lanes)
                totals = [[None] * 3 for _ in range(per_device)]
                for t in range(slot_tiles):
                    pull = weight[t * TILE : (t + 1) * TILE, lanes]
                    for b in range(per_device):
                        offsets = []
                        for c in range(3):
                            sides = [
                                ghost_row(ghost_ref_of, ghost_lead, side, c, b) for side in range(2)
                            ]
                            found = found_near[found_at(m, b, c, t), :]
                            offsets.append(
                                pick_ghost(sides, found, lows[t], highs[t])
                                - own_row(own_ref, own_lead, m, c, b)
                            )
                        squared = sum(offset * offset for offset in offsets)
                        strength = pull * jnp.exp(-squared / pair_width)
                        for c in range(3):
                            term = strength * offsets[c]
                            totals[b][c] = term if t == 0 else totals[b][c] + term
                for b in range(per_device):
                    at = h * per_device + b
                    for c in range(3):
                        total = jnp.sum(totals[b][c], axis=0, keepdims=True)
                        kick[at : at + 1, lane_of(s, c)] = pair_strength * factor * total
            finish(s)

    def share_lanes(t):
        return pl.ds(pl.multiple_of(first + t * LANES, LANES), LANES)

    def q_at(t, c, k):
        at = ((t * 3 + c) * slot_tiles + k) * TILE
        return slice(at, at + TILE)

    def learned_own():
        for t in range(cover // LANES):
            lows, highs = near_tiles(share_lanes(t))
            for k in range(slot_tiles):
                for c in range(3):
                    sources = [spread_row(q_own[c : c + 1, chunk_of(m)]) for m in range(atom_chunks)]
                    found_q[q_at(t, c, k), :] = pick_own(sources, lows[k], highs[k])

    def learned(low_high, slot):
        rates = radial_rates(w_in_ref.shape[0])
        forces, lines, held = [], [], []
        for t in range(cover // LANES):
            lanes = share_lanes(t)
            lows, highs = near_tiles(lanes)
            offsets = [[None] * slot_tiles for _ in range(3)]
            for k in range(slot_tiles):
                for c in range(3):
                    found = pick_ghost(low_high(c), found_q[q_at(t, c, k), :], lows[k], highs[k])
                    offsets[c][k] = found - spread_row(q_own[c : c + 1, lanes])
            bases = []
            messages = [None] * len(rates)
            for k in range(slot_tiles):
                squared = sum(offsets[c][k] * offsets[c][k] for c in range(3))
                basis = [jnp.exp(-float(rates[r]) * squared) for r in range(2)]
                for r in range(2, len(rates)):
                    basis.append(basis[r - 2] * basis[r - 2])
                bases.append(basis)
                strength = weight[k * TILE : (k + 1) * TILE, lanes]
                for r in range(len(rates)):
                    term = strength * basis[r]
                    messages[r] = term if messages[r] is None else messages[r] + term
            lines.append(jnp.concatenate(
                [jnp.sum(m, axis=0, keepdims=True) for m in messages], axis=0
            ) / slots)
            held.append((offsets, bases))
        hidden = lax.dot_general(
            w_in_ref[...], jnp.concatenate(lines, axis=1), (((0,), (0,)), ((), ())),
            precision=highest, preferred_element_type=jnp.float32,
        )
        hidden = hidden * jax.nn.sigmoid(hidden)
        radials = dot(w_out_ref[...], hidden)
        for t in range(cover // LANES):
            lanes = share_lanes(t)
            offsets, bases = held[t]
            radial = radials[:, t * LANES : (t + 1) * LANES]
            spread_radial = [spread_row(radial[r : r + 1, :]) for r in range(len(rates))]
            totals = [None] * 3
            for k in range(slot_tiles):
                profile = sum(spread_radial[r] * bases[k][r] for r in range(len(rates)))
                strength = weight[k * TILE : (k + 1) * TILE, lanes] * profile
                for c in range(3):
                    term = strength * offsets[c][k]
                    totals[c] = term if totals[c] is None else totals[c] + term
            tile = jnp.zeros((TILE, LANES), jnp.float32)
            for c in range(3):
                total = spread_row(jnp.sum(totals[c], axis=0, keepdims=True))
                tile = jnp.where(row_at % 4 == c, total, tile)
            forces.append(tile)
            tile = jnp.where(row_at // 4 == t % 2, tile, 0.0)
            at = t // 2 * TILE
            if t % 2:
                tile = tile + piece[slot, me, at : at + TILE, :]
            piece[slot, me, at : at + TILE, :] = tile
        if slot == 0:
            begins = lax.rem(me, groups) * share
            for side in range(2):
                index = spread_row(ghost_ref[1 - side : 2 - side, :])
                low, high = index & (LANES - 1), index // LANES
                value = jnp.zeros((TILE, LANES), jnp.float32)
                for t in range(cover // LANES):
                    force = forces[t] * spread_row(inv_row[:, share_lanes(t)])
                    value = jnp.where(high == first // LANES + t, lookup(force, low), value)
                value = jnp.where((index >= begins) & (index < begins + share), value, 0.0)
                side_out[side] = value[0:4]
            send_around(side_out, side_in, side_at)
        send_peers(lambda j: piece.at[slot, me], piece.at[slot, me], piece_at + slot)

    def all_pieces(slot, scale):
        line = []
        for s in range(strips):
            for i in range(3):
                tiles = []
                for top in range(0, extra, TILE):
                    tile = jnp.zeros((TILE, LANES), jnp.float32)
                    for row in range(top, min(extra, top + TILE)):
                        h, c = row // CB, row % CB
                        m = h * strips + s
                        source = c * groups + m * LANES // share
                        t = (m * LANES - (source % groups) * share // LANES * LANES) // LANES
                        at = t // 2 * TILE + t % 2 * 4 + i
                        value = piece[slot, source, at : at + 1, :]
                        if scale is not None:
                            value = value * scale[:, chunk_of(m)]
                        tile = jnp.where(row_at == row - top, spread_row(value), tile)
                    tiles.append(tile)
                line.append(jnp.concatenate(tiles, axis=0))
        return jnp.concatenate(line, axis=1)

    def send_kick(step):
        def finish(s):
            lanes = slice(s * wide, (s + 1) * wide)
            if step == 0:
                kicks[0, me, :, lanes] = first_vel[:, lanes] + (0.5 * inner_step) * kick[:, lanes]
            else:
                kick[:, lanes] = inner_step * kick[:, lanes]
                kicks[step, me, :, lanes] = kick[:, lanes]
            strip = kicks.at[step, me, :, lanes]
            send_peers(lambda j: strip, strip, kick_at + step)
        return finish

    base_row = extra + TILE
    step_row = [base_row + KINDS * TILE]
    for step in range(NINNER):
        step_row.append(step_row[-1] + (KINDS - step) * TILE)

    free_kinds = ((0, per_device), (1, per_device), (2, per_device), (4, 1))

    def send_edges(step):
        if step == 0:
            kick[...] = kicks[0, me]
        for side in range(2):
            tiles = compose(ghost_values(kick, (), side, per_device), per_device)
            for t, tile in enumerate(tiles):
                rows = min(TILE, 3 * per_device - t * TILE)
                edge_out[step, side, t * TILE : t * TILE + rows, :] = tile[0:rows]
        send_around(edge_out.at[step], edge_in.at[step], edge_at + step)

    def await_edges(step):
        arrived(edge_in.at[step], edge_at + step)
        if step == 0:
            arrived(side_in, side_at)
            arrived(free_in, free_at)
            for side in range(2):
                for c in range(CB):
                    total = side_in[side, c * groups]
                    for part in range(1, groups):
                        total = total + side_in[side, c * groups + part]
                    side_sum[side, c] = total
        lines = []
        for side in range(2):
            for t in range(ghost_tiles):
                rows = min(TILE, 3 * per_device - t * TILE)
                tiles = []
                for device in range(devices):
                    tile = edge_in[step, side, device, t * TILE : t * TILE + rows, :]
                    if rows < TILE:
                        tile = jnp.concatenate(
                            (tile, jnp.zeros((TILE - rows, LANES), jnp.float32)), axis=0
                        )
                    tiles.append(tile)
                if step == 0:
                    for top in range(0, extra, TILE):
                        tile = jnp.zeros((TILE, LANES), jnp.float32)
                        for row in range(top, min(extra, top + TILE)):
                            i, c = t * groups_of + row // CB, row % CB
                            if i < 3:
                                value = spread_row(side_sum[side, c, i : i + 1, :])
                                tile = jnp.where(row_at == row - top, value, tile)
                        tiles.append(tile)
                lines.append(jnp.concatenate(tiles, axis=0))
        return jnp.concatenate(lines, axis=1)

    for load in loads[7:]:
        load.wait()
    cheap_own(first_pos, ())
    arrived(others(part_in), part_at)
    contracted = part_out[member]
    for j in order:
        contracted = contracted + part_in[peers[j]]
    part_line[0 : contracted.shape[0], 0:LANES] = contracted

    def put_q(value_of):
        for i in range(3):
            for m in range(atom_chunks):
                q_own[i : i + 1, chunk_of(m)] = value_of(i, m)

    put_q(lambda i, m: part_line[i * atom_chunks + m : i * atom_chunks + m + 1, 0:LANES])
    for side in range(2):
        low, high = index_of(side)
        qg_out[side] = pick([q_own[:, chunk_of(m)] for m in range(atom_chunks)], low, high)[0:4]
    send_sides(qg_out, qg_in, qghost_at)
    learned_own()
    arrived(zg_in, ghost_at)

    chunks = [ghost_row(zg_in, (), 0, 3, 0)]
    chunks += [spread_row(charge[:, chunk_of(m)]) for m in range(atom_chunks)]
    chunks += [ghost_row(zg_in, (), 1, 3, 0)]
    for m in range(atom_chunks):
        itself = ghosts + m * LANES + lax.broadcasted_iota(jnp.int32, (TILE, LANES), 1)
        for k in range(0, slots, TILE):
            index = near_ref[k : k + TILE, chunk_of(m)]
            value = pick(chunks, index & (LANES - 1), index // LANES)
            weight[k : k + TILE, chunk_of(m)] = jnp.where(index == itself, 0.0, value)

    cheap(first_pos, (), zg_in, (), send_kick(0))
    send_edges(0)
    arrived(others(begin), begin_at)
    based = dot(table_ref[base_row : base_row + KINDS * TILE, 0:width], begin[...].reshape(width, -1))
    for kind in range(KINDS):
        acc[kind] = based[kind * TILE : (kind + 1) * TILE, :]
    for side in range(2):
        for number, (kind, unit) in enumerate(free_kinds):
            for t, tile in enumerate(compose(ghost_values(acc, (kind,), side, unit), unit)):
                at = (number * ghost_tiles + t) * TILE
                free_out[side, at : at + TILE, :] = tile
    send_sides(free_out, free_in, free_at)
    arrived(qg_in, qghost_at)
    learned(lambda c: [spread_row(qg_in[side, c : c + 1, :]) for side in range(2)], 0)

    for step in range(NINNER):
        last = step + 1 == NINNER
        arrived(others(kicks.at[step]), kick_at + step)
        every = kicks[step].reshape(width, -1)
        depth = width
        if step == 0:
            arrived(others(piece.at[0]), piece_at)
            every = jnp.concatenate((every, all_pieces(0, inverse)), axis=0)
            depth = width + extra
        table = table_ref[step_row[step] : step_row[step + 1], 0:depth]
        moved = dot(table, every)
        for kind in range(step, KINDS):
            at = (kind - step) * TILE
            acc[kind] = acc[kind] + moved[at : at + TILE, :]
        if last:
            put_q(lambda i, m: acc[4, m // strips : m // strips + 1, lane_of(m % strips, i)])
            learned_own()
        else:
            cheap_own(acc, (step,))
        moved = dot(table, await_edges(step))
        for side in range(2):
            for number, (kind, _) in enumerate(free_kinds):
                if kind < step:
                    continue
                at = (kind - step) * TILE
                for t in range(ghost_tiles):
                    line = (side * ghost_tiles + t) * LANES
                    held = slice((number * ghost_tiles + t) * TILE, (number * ghost_tiles + t + 1) * TILE)
                    old = free_in if step == 0 else ghost_acc
                    ghost_acc[side, held, :] = (
                        old[side, held, :] + moved[at : at + TILE, line : line + LANES]
                    )
        if last:
            def low_high(c):
                at = (3 * ghost_tiles + c // groups_of) * TILE + c % groups_of
                return [spread_row(ghost_acc[side, at : at + 1, :]) for side in range(2)]

            learned(low_high, 1)
        shifted = ghost_acc.at[:, step * ghost_tiles * TILE : (step + 1) * ghost_tiles * TILE, :]
        if last:
            cheap_own(acc, (step,))
            cheap(acc, (step,), shifted, (), lambda s: None)
        else:
            cheap(acc, (step,), shifted, (), send_kick(step + 1))
            send_edges(step + 1)

    for h in range(halves):
        at = slice(h * per_device, (h + 1) * per_device)
        for s in range(strips):
            for c in range(3):
                new_ref[0, c, :, chunk_of(h * strips + s)] = acc[2, at, lane_of(s, c)]
    for copy in sent:
        copy.wait_send()
    arrived(others(piece.at[1]), piece_at + 1)
    slow = dot(table_ref[extra : extra + TILE, 0:extra], all_pieces(1, None))
    for s in range(strips):
        heavy = mass_rows[:, chunk_of(s)]
        for c in range(3):
            lanes = lane_of(s, c)
            kick[:, lanes] = (
                acc[3, :, lanes] + (0.5 * inner_step) * kick[:, lanes]
            ) * heavy + slow[:, lanes]
    for h in range(halves):
        at = slice(h * per_device, (h + 1) * per_device)
        for s in range(strips):
            for c in range(3):
                new_ref[1, c, :, chunk_of(h * strips + s)] = kick[at, lane_of(s, c)]
    sent[-1].wait_send()


def body(
    positions, momenta, neighbours, ghost_rows, species, species_scale, mass_table, w_in, w_out
):
    per_device, _, atoms = positions.shape
    slots = neighbours.shape[0]
    ghosts = ghost_rows.shape[0] // 2
    devices = lax.axis_size("bead")
    table = tables(devices, per_device, atoms)
    groups_of, halves, strips = layout(devices, per_device, atoms)
    ghost_tiles = -(-3 // groups_of)
    extra = halves * CB
    lanes = 3 * LANES * strips
    cover = max(atoms // (devices // CB), LANES)
    lines = 3 * (atoms // LANES)
    piece_rows = -(-(cover // LANES) // 2) * TILE
    vmem = pl.BlockSpec(memory_space=pltpu.VMEM)
    hbm = pl.BlockSpec(memory_space=pltpu.HBM)
    f32 = jnp.float32
    dma = pltpu.SemaphoreType.DMA
    operands = (
        positions.transpose(1, 0, 2), momenta.transpose(1, 0, 2), neighbours,
        ghost_rows.reshape(2, ghosts), species.reshape(1, atoms), species_scale.reshape(1, -1),
        mass_table.reshape(1, -1), w_in.T, w_out, table,
    )
    shape = jax.ShapeDtypeStruct((2, *operands[0].shape), f32)
    new = pl.pallas_call(
        cycle_kernel,
        name="cycle",
        out_shape=shape,
        in_specs=[hbm] * 10,
        out_specs=vmem,
        scratch_shapes=[
            pltpu.VMEM((TILE, lanes), f32),
            pltpu.VMEM((TILE, lanes), f32),
            pltpu.VMEM((TILE, strips * LANES), f32),
            pltpu.VMEM((1, atoms), f32),
            pltpu.VMEM((TILE, strips * LANES), f32),
            pltpu.VMEM((slots, atoms), f32),
            pltpu.VMEM((TILE, lanes), f32),
            pltpu.VMEM((KINDS, TILE, lanes), f32),
            pltpu.VMEM((2, 4 * ghost_tiles * TILE, ghosts), f32),
            pltpu.VMEM((devices, TILE, lanes), f32),
            pltpu.VMEM((NINNER, devices, TILE, lanes), f32),
            pltpu.VMEM((2, ghost_tiles * TILE, ghosts), f32),
            pltpu.VMEM((2, ghost_tiles * TILE, ghosts), f32),
            pltpu.VMEM((max(extra, -(-lines // TILE) * TILE), lanes), f32),
            pltpu.VMEM((CB, lines, LANES), f32),
            pltpu.VMEM((devices, lines, LANES), f32),
            pltpu.VMEM((TILE, atoms), f32),
            pltpu.VMEM((2, 4, ghosts), f32),
            pltpu.VMEM((2, 4, ghosts), f32),
            pltpu.VMEM((2, devices, piece_rows, LANES), f32),
            pltpu.VMEM((2, 4 * ghost_tiles * TILE, ghosts), f32),
            pltpu.VMEM((2, 4 * ghost_tiles * TILE, ghosts), f32),
            pltpu.VMEM((NINNER, 2, 3 * per_device, ghosts), f32),
            pltpu.VMEM((NINNER, 2, devices, 3 * per_device, ghosts), f32),
            pltpu.VMEM((2, 4, ghosts), f32),
            pltpu.VMEM((2, devices, 4, ghosts), f32),
            pltpu.VMEM((2, CB, 4, ghosts), f32),
            pltpu.VMEM((atoms // LANES * per_device * 3 * slots, LANES), f32),
            pltpu.VMEM((cover // LANES * 3 * slots, LANES), f32),
            pltpu.VMEM((1, atoms), f32),
            *[pltpu.VMEM(operand.shape, operand.dtype) for operand in operands[:-1]],
            pltpu.VMEM(table.shape[1:], f32),
            dma((len(operands),)),
            dma((8 + 2 * NINNER,)), dma((8 + 2 * NINNER,)),
        ],
        compiler_params=pltpu.CompilerParams(
            collective_id=0, has_side_effects=True, vmem_limit_bytes=16777216
        ),
    )(*[pltpu.with_memory_space_constraint(x, pltpu.HBM) for x in operands])
    return (new[0].transpose(1, 0, 2), new[1].transpose(1, 0, 2))


def solution(mesh):
    in_specs = (
        P("bead", None, "space"),
        P("bead", None, "space"),
        P(None, "space"),
        P("space"),
        P("space"),
        P(),
        P(),
        P(),
        P(),
    )
    out_specs = (P("bead", None, "space"), P("bead", None, "space"))
    return jax.shard_map(body, mesh=mesh, in_specs=in_specs, out_specs=out_specs, check_vma=False)
```
